256 devices in a mesh: leaf: 4 (over x), row: 8 (over z_lo, core), col: 8 (over z_hi, y).
Axes of the slice: x: 4, y: 4, z: 8 (z_hi: 2, z_lo: 4; z = z_hi * 4 + z_lo), core: 2. Of those that a mesh axis runs over, the one named last changes fastest.
Arguments:
- root_inverse: float32 [4096, 4096], P('row', ('leaf', 'col')), may hold values from -48 to 48, as said below
- lower_panel: float32 [4, 4096, 4096], P('leaf', 'row', 'col'), may hold values from -0.375 to 0.375
- panel_mask: int32 [4, 16, 16], P('leaf', 'row', 'col'), may hold values from 0 to 1, as said below
- factor_inverse: float32 [4, 4096, 4096], P('leaf', 'row', 'col'), may hold values from -8 to 8, as said below
Outputs:
- cross_inverse: float32 [4, 4096, 4096], P('leaf', 'row', 'col')
- block_inverse: float32 [4, 4096, 4096], P('leaf', 'row', 'col')
The draws below stay inside these ranges and needn't reach their ends.
Inputs may be any that keep to these rules, and one draw needn't show every extreme that they name: `panel_mask`: each entry says whether the 256 x 256 block of a child's panel is kept; the share of kept blocks differs from block row to block row. `root_inverse`: symmetric and positive definite. `factor_inverse`: each child's matrix is symmetric and positive definite.
All inputs are finite; a program needn't handle non-finite values.
Results may differ from the reference program's by a relative error of at most 0.0001.
Values sent between devices are 32-bit elements; how exact they have to be, the bound alone decides.
No kernel may reach another device: no remote copies, remote signals or barrier semaphores. Data moves between devices by JAX's collectives and lax.ppermute only.
A program may use at most 192 MiB of HBM per device.

```python
import math
import jax
import jax.numpy as jnp
from jax import lax

BS = 256
NR = 4096
NC = 4096
CHILDREN = 4
RB = 16
CB = 16


def draw_root_inverse(key, part):
    keys = jax.random.split(key, 2)
    raw = jax.random.truncated_normal(keys[0], -6.0, 6.0, (NR, NR), jnp.float32)
    coupling = (raw + raw.T) * (0.35 / math.sqrt(NR))
    identity = (lax.broadcasted_iota(jnp.int32, (NR, NR), 0) == lax.broadcasted_iota(jnp.int32, (NR, NR), 1)).astype(jnp.float32)
    diagonal = jax.random.uniform(keys[1], (NR,), jnp.float32, 1.5, 3.0)
    matrix = coupling * (1.0 - identity) + identity * diagonal[None, :]
    return matrix


def draw_factor_inverse(key, part):
    keys = jax.random.split(key, 2)
    raw = jax.random.truncated_normal(keys[0], -6.0, 6.0, (CHILDREN, NC, NC), jnp.float32)
    coupling = (raw + jnp.swapaxes(raw, 1, 2)) * (0.2 / math.sqrt(NC))
    identity = (lax.broadcasted_iota(jnp.int32, (1, NC, NC), 1) == lax.broadcasted_iota(jnp.int32, (1, NC, NC), 2)).astype(jnp.float32)
    diagonal = jax.random.uniform(keys[1], (CHILDREN, 1, NC), jnp.float32, 1.0, 2.0)
    matrix = coupling * (1.0 - identity) + identity * diagonal
    return matrix


def draw_panel_mask(key, part):
    keys = jax.random.split(key, 2)
    level = jax.random.randint(keys[0], (CHILDREN, RB, 1), 0, 9)
    coins = jax.random.randint(keys[1], (CHILDREN, RB, CB), 0, 8)
    return (coins < level).astype(jnp.int32)


def level_of(key, shape, shards, least, high):
    level, own = 1.0, jax.random.fold_in(key, 6)
    for position, shards_of in shards:
        steps = jnp.exp(jax.random.uniform(jax.random.fold_in(own, position), (shards_of,), jnp.float32, least / len(shards), high / len(shards)))
        level = level * jnp.repeat(steps, shape[position] // shards_of).reshape([-1 if axis == position else 1 for axis in range(len(shape))])
    return level


def bell_draw(own_key, dims, width, most, cuts=(), kind=jnp.bfloat16):
    entries = width * jax.random.normal(own_key, dims, jnp.float32)
    if cuts:
        entries = entries * level_of(own_key, dims, cuts, -0.22, 0.18)
    return jnp.clip(entries, -most, most).astype(kind)


def setup_inputs(seed: int = 0) -> dict:
    arg_keys = jax.random.split(jax.random.key(seed), 5)
    return {
        "root_inverse": draw_root_inverse(jax.random.fold_in(arg_keys[4], 71), 0),
        "lower_panel": bell_draw(arg_keys[1], (CHILDREN, NR, NC), (NR // 16) ** -0.5, 0.375, ((0, 4), (1, 8), (2, 8)), jnp.float32),
        "panel_mask": draw_panel_mask(jax.random.fold_in(arg_keys[4], 71), 0),
        "factor_inverse": draw_factor_inverse(jax.random.fold_in(arg_keys[4], 71), 0),
    }


def spread(mask):
    return jnp.repeat(jnp.repeat(mask.astype(jnp.float32), BS, axis=1), BS, axis=2)


def reference(root_inverse, lower_panel, panel_mask, factor_inverse):
    pattern = spread(panel_mask)
    masked = lower_panel * pattern
    crosses = []
    blocks = []
    for kid_index in range(CHILDREN):
        ancestor = jnp.dot(root_inverse, masked[kid_index], precision=lax.Precision.HIGHEST, preferred_element_type=jnp.float32)
        crosses.append(-(ancestor * pattern[kid_index]))
        blocks.append(factor_inverse[kid_index] + jnp.dot(masked[kid_index].T, ancestor, precision=lax.Precision.HIGHEST, preferred_element_type=jnp.float32))
    return jnp.stack(crosses), jnp.stack(blocks)
```

```python
import jax
import jax.numpy as jnp
from jax import lax
from jax.sharding import Mesh
from jax.sharding import PartitionSpec as P

AXES = ("leaf", "z_lo", "core", "z_hi", "y")
COL = ("z_hi", "y")
NX, NL, NH, NY = 4, 4, 2, 4
NZ = NL * NH
HIGH = lax.Precision.HIGH


def way(core):
    return 1 if core == 0 else -1


def z_step(block):
    def place(z, core):
        return ((z % NL) * 2 + core) * NH + z // NL

    pairs = [(place(z, core), place((z + way(core)) % NZ, core)) for z in range(NZ) for core in range(2)]
    return lax.ppermute(block, ("z_lo", "core", "z_hi"), pairs)


def y_step(block):
    pairs = [(core * NY + y, core * NY + (y + way(core)) % NY) for y in range(NY) for core in range(2)]
    return lax.ppermute(block, ("core", "y"), pairs)


def x_step(block):
    pairs = [(x * 2 + core, (x + way(core)) % NX * 2 + core) for x in range(NX) for core in range(2)]
    return lax.ppermute(block, ("leaf", "core"), pairs)


def swap(block, axis):
    return lax.ppermute(block, axis, [(0, 1), (1, 0)])


def spread(mask, rows, cols):
    mask = mask.astype(jnp.float32)
    low = lax.broadcasted_iota(jnp.int32, (rows, cols), 0) < rows // 2
    left = lax.broadcasted_iota(jnp.int32, (rows, cols), 1) < cols // 2
    return jnp.where(low, jnp.where(left, mask[0, 0], mask[0, 1]), jnp.where(left, mask[1, 0], mask[1, 1]))


def put(array, block, *starts):
    return lax.dynamic_update_slice(array, block, starts)


def per_device(root_inverse, lower_panel, panel_mask, factor_inverse):
    x, zl, core, zh, y = (lax.axis_index(name) for name in AXES)
    z = zh * NL + zl
    turn = 1 - 2 * core
    n = lower_panel.shape[1]
    q = root_inverse.shape[1]
    pattern = spread(panel_mask[0], n, n)
    mine = lower_panel[0] * pattern

    def across_y(part):
        wide = jnp.zeros((n, NY * q), jnp.float32)
        for t in range(NY):
            wide = put(wide, part, 0, (y - turn * t) % NY * q)
            if t < NY - 1:
                part = y_step(part)
        return wide

    root = jnp.zeros((n, NX * NH * n), jnp.float32)
    for half, part in ((zh, root_inverse), (1 - zh, swap(root_inverse, "z_hi"))):
        part = across_y(part)
        for t in range(NX):
            root = put(root, part, 0, ((x - turn * t) % NX * NH + half) * n)
            if t < NX - 1:
                part = x_step(part)

    panel = jnp.zeros((NL * 2 * n, NH * n), jnp.float32)
    ring = [mine]
    for s in range(NZ):
        if s:
            ring.append(z_step(ring[-1]))
        for block, from_z, from_core in (
            (ring[-1], (z - turn * s) % NZ, core),
            (swap(ring[-1], "core"), (z + turn * s) % NZ, 1 - core),
        ):
            panel = put(panel, block, (from_z % NL * 2 + from_core) * n, from_z // NL * n)

    rows = jnp.zeros((n, NH * NY * n), jnp.float32)
    for half, part in ((zh, mine), (1 - zh, ring[NL])):
        for t in range(NY):
            rows = put(rows, part, 0, (half * NY + (y - turn * t) % NY) * n)
            if t < NY - 1:
                part = y_step(part)

    ancestor = jnp.dot(root, panel, precision=HIGH, preferred_element_type=jnp.float32)
    cross = -(lax.dynamic_slice(ancestor, (0, zh * n), (n, n)) * pattern)

    def partial(to_z, to_core):
        left = lax.dynamic_slice(rows, (0, (to_z % NL * 2 + to_core) * n), (n, n))
        right = lax.dynamic_slice(ancestor, (0, to_z // NL * n), (n, n))
        return lax.dot_general(
            left, right, (((0,), (0,)), ((), ())), precision=HIGH, preferred_element_type=jnp.float32
        )

    total = None
    for d in range(NL - 1, -1, -1):
        theirs = swap(partial((z - turn * d) % NZ, 1 - core), "core")
        own = partial((z + turn * d) % NZ, core) + theirs
        total = own if total is None else z_step(total) + own
    return cross[None], factor_inverse + total[None]


def solution(mesh):
    split = Mesh(mesh.devices.reshape(NX, NL, 2, NH, NY), AXES)
    row = ("z_lo", "core")
    block = P("leaf", row, COL)
    return jax.shard_map(
        per_device,
        mesh=split,
        in_specs=(P(row, ("leaf",) + COL), block, block, block),
        out_specs=(block, block),
        check_vma=False,
    )
```

```python
import functools

import jax
import jax.numpy as jnp
from jax import lax
from jax.experimental import pallas as pl
from jax.experimental.pallas import tpu as pltpu
from jax.sharding import Mesh
from jax.sharding import PartitionSpec as P

AXES = ("leaf", "z_lo", "core", "z_hi", "y")
COL = ("z_hi", "y")
NX, NL, NH, NY = 4, 4, 2, 4
NZ = NL * NH
ANY = pl.BlockSpec(memory_space=pl.ANY)
SMEM = pl.BlockSpec(memory_space=pltpu.SMEM)


def way(core):
    return 1 if core == 0 else -1


def z_step(block):
    def place(z, core):
        return ((z % NL) * 2 + core) * NH + z // NL

    pairs = [(place(z, core), place((z + way(core)) % NZ, core)) for z in range(NZ) for core in range(2)]
    return lax.ppermute(block, ("z_lo", "core", "z_hi"), pairs)


def y_step(block):
    pairs = [(core * NY + y, core * NY + (y + way(core)) % NY) for y in range(NY) for core in range(2)]
    return lax.ppermute(block, ("core", "y"), pairs)


def x_step(block):
    pairs = [(x * 2 + core, (x + way(core)) % NX * 2 + core) for x in range(NX) for core in range(2)]
    return lax.ppermute(block, ("leaf", "core"), pairs)


def swap(block, axis):
    return lax.ppermute(block, axis, [(0, 1), (1, 0)])


def spread(mask, rows, cols):
    mask = mask.astype(jnp.float32)
    low = lax.broadcasted_iota(jnp.int32, (rows, cols), 0) < rows // 2
    left = lax.broadcasted_iota(jnp.int32, (rows, cols), 1) < cols // 2
    return jnp.where(low, jnp.where(left, mask[0, 0], mask[0, 1]), jnp.where(left, mask[1, 0], mask[1, 1]))


def split(value):
    high = value.astype(jnp.bfloat16)
    return high, (value - high.astype(jnp.float32)).astype(jnp.bfloat16)


def product(left, right):
    left_high, left_low = split(left)
    right_high, right_low = split(right)
    dot = functools.partial(jnp.dot, preferred_element_type=jnp.float32)
    return dot(left_high, right_high) + (dot(left_high, right_low) + dot(left_low, right_high))


def fetch(index, refs, buffer, sem):
    for i, ref in enumerate(refs):

        @pl.when(index == i)
        def _():
            pltpu.make_async_copy(ref, buffer, sem).start()


def params(mib):
    return pltpu.CompilerParams(vmem_limit_bytes=mib << 20)


def cost(dots, n):
    return pl.CostEstimate(flops=6 * dots * n**3, bytes_accessed=12 * dots * n * n, transcendentals=0)


def gather_kernel(steps, lefts, rights, fresh, *refs):
    table, refs = refs[0], refs[1:]
    left, refs = refs[:lefts], refs[lefts:]
    right, refs = refs[:rights], refs[rights:]
    if not fresh:
        before, refs = refs[0], refs[1:]
    after, left_buffer, right_buffer, total, left_sems, right_sems, sem = refs

    def start(s, slot):
        fetch(table[s, 0], left, left_buffer.at[slot], left_sems.at[slot])
        fetch(table[s, 1], right, right_buffer.at[slot], right_sems.at[slot])

    start(0, 0)
    if fresh:
        total[...] = jnp.zeros_like(total)
    else:
        load = pltpu.make_async_copy(before, total, sem)
        load.start()
        load.wait()

    @pl.loop(0, steps)
    def _(s):
        slot = lax.rem(s, 2)

        @pl.when(s + 1 < steps)
        def _():
            start(s + 1, 1 - slot)

        pltpu.make_async_copy(left[0], left_buffer.at[slot], left_sems.at[slot]).wait()
        pltpu.make_async_copy(right[0], right_buffer.at[slot], right_sems.at[slot]).wait()
        half = table[s, 2]
        total[half] = total[half] + product(left_buffer[slot], right_buffer[slot])

    store = pltpu.make_async_copy(total, after, sem)
    store.start()
    store.wait()


def accumulate(table, left, right, total):
    n = left[0].shape[0]
    fresh = total is None
    steps = table.shape[0]
    operands = [table, *left, *right] + ([] if fresh else [total])
    block = pltpu.VMEM((2, n, n), jnp.float32)
    pair = pltpu.SemaphoreType.DMA((2,))
    return pl.pallas_call(
        functools.partial(gather_kernel, steps, len(left), len(right), fresh),
        out_shape=jax.ShapeDtypeStruct((2, n, n), jnp.float32),
        in_specs=[SMEM] + [ANY] * (len(operands) - 1),
        out_specs=ANY,
        scratch_shapes=[block, block, block, pair, pair, pltpu.SemaphoreType.DMA],
        input_output_aliases={} if fresh else {len(operands) - 1: 0},
        compiler_params=params(24),
        cost_estimate=cost(steps, n),
    )(*operands)


def pair_kernel(lefts, table, *refs):
    left, (right, own, theirs, left_buffer, right_buffer, left_sems, right_sems) = refs[:lefts], refs[lefts:]
    for k in range(2):
        fetch(table[k, 0], left, left_buffer.at[k], left_sems.at[k])
        pltpu.make_async_copy(right.at[table[k, 1]], right_buffer.at[k], right_sems.at[k]).start()
    for k, out in enumerate((theirs, own)):
        pltpu.make_async_copy(left[0], left_buffer.at[k], left_sems.at[k]).wait()
        pltpu.make_async_copy(right.at[table[k, 1]], right_buffer.at[k], right_sems.at[k]).wait()
        out[...] = product(left_buffer[k], right_buffer[k])


def partial_pair(table, left, right):
    n = left[0].shape[0]
    block = pltpu.VMEM((2, n, n), jnp.float32)
    pair = pltpu.SemaphoreType.DMA((2,))
    whole = pl.BlockSpec(memory_space=pltpu.VMEM)
    out = jax.ShapeDtypeStruct((n, n), jnp.float32)
    return pl.pallas_call(
        functools.partial(pair_kernel, len(left)),
        out_shape=(out, out),
        in_specs=[SMEM] + [ANY] * (len(left) + 1),
        out_specs=(whole, whole),
        scratch_shapes=[block, block, pair, pair],
        compiler_params=params(24),
        cost_estimate=cost(2, n),
    )(table, *left, right)


def per_device(root_inverse, lower_panel, panel_mask, factor_inverse):
    x, zl, core, zh, y = (lax.axis_index(name) for name in AXES)
    z = zh * NL + zl
    turn = 1 - 2 * core
    n = lower_panel.shape[1]
    q = root_inverse.shape[1]
    pattern = spread(panel_mask[0], n, n)
    mine = lower_panel[0] * pattern

    def root_across_y(part):
        wide = jnp.zeros((n, NY * q), jnp.float32)
        for t in range(NY):
            wide = lax.dynamic_update_slice(wide, part, (0, (y - turn * t) % NY * q))
            if t < NY - 1:
                part = y_step(part)
        return wide

    s = jnp.arange(NZ)
    same = (core == zh).astype(jnp.int32)

    def meet(direct):
        from_z = (z - turn * s * (2 * direct - 1)) % NZ
        return (turn * (x - from_z % NL)) % NX, 1 - direct, from_z // NL

    near_root, near_ring, near_half = meet(same)
    far_root, far_ring, far_half = meet(1 - same)

    def table_of(root, ring, half, steps, first):
        return jnp.stack([root[first : first + steps], ring * steps + jnp.arange(steps), half[first : first + steps]], 1)

    ring, other = [mine], []
    root_far = swap(root_inverse, "z_hi")
    ring.append(z_step(mine))
    near = [root_across_y(root_inverse)]
    mine_t = mine.T
    rows_near = [mine_t]
    rows_far = []
    far = []
    (ring[1], near[0], root_far) = lax.optimization_barrier((ring[1], near[0], root_far))
    other.append(swap(mine, "core"))
    ring.append(z_step(ring[1]))
    near.append(x_step(near[0]))
    far.append(root_across_y(root_far))
    ring[2], near[1], far[0], other[0] = lax.optimization_barrier((ring[2], near[1], far[0], other[0]))
    for r in range(3, NZ):
        other.append(swap(ring[r - 2], "core"))
        ring.append(z_step(ring[r - 1]))
        (near if r < 5 else far).append(x_step((near if r < 5 else far)[-1]))
        rows = rows_near if r < 6 else rows_far
        rows.append(y_step(rows[-1]))
        ring[-1], other[-1], moved, rows[-1] = lax.optimization_barrier(
            (ring[-1], other[-1], (near if r < 5 else far)[-1], rows[-1])
        )
        (near if r < 5 else far)[-1] = moved
        if r == 5:
            rows_far.append(ring[NL].T)
    other.append(swap(ring[NZ - 2], "core"))
    other.append(swap(ring[NZ - 1], "core"))
    rows_far.append(y_step(rows_far[-1]))

    first = NL + 1
    total = accumulate(
        table_of(near_root, near_ring, near_half, first, 0), near, ring[:first] + other[:first], None
    )
    rest = NZ - 1 - first
    total = accumulate(
        table_of(near_root, near_ring, near_half, rest, first), near, ring[first:-1] + other[first:-1], total
    )
    total = accumulate(table_of(far_root, far_ring, far_half, NZ - 1, 0), far, ring[:-1] + other[:-1], total)
    last = jnp.concatenate(
        [table_of(near_root, near_ring, near_half, 1, NZ - 1), table_of(far_root + NX, far_ring, far_half, 1, NZ - 1)]
    )
    total = accumulate(last, near + far, [ring[-1], other[-1]], total)
    cross = -(lax.dynamic_index_in_dim(total, zh, 0, False) * pattern)

    rows = rows_near + rows_far
    d = jnp.arange(NL)[:, None]
    sign = jnp.array([[-1, 1]])
    to_z = (z + turn * sign * d) % NZ
    to_core = jnp.where(sign > 0, core, 1 - core)
    block = to_z % NL * 2 + to_core
    step = (turn * (y - block % NY)) % NY
    table = jnp.stack([jnp.where(block // NY == zh, step, step + NY), to_z // NL], 2)
    parts = [partial_pair(table[k], rows, total) for k in range(NL)]
    reduced = None
    for own, theirs in parts[::-1]:
        own = own + swap(theirs, "core")
        reduced = own if reduced is None else z_step(reduced) + own
    return cross[None], factor_inverse + reduced[None]


def solution(mesh):
    split_mesh = Mesh(mesh.devices.reshape(NX, NL, 2, NH, NY), AXES)
    row = ("z_lo", "core")
    block = P("leaf", row, COL)
    return jax.shard_map(
        per_device,
        mesh=split_mesh,
        in_specs=(P(row, ("leaf",) + COL), block, block, block),
        out_specs=(block, block),
        check_vma=False,
    )
```

```python
import functools

import jax
import jax.numpy as jnp
from jax import lax
from jax.experimental import pallas as pl
from jax.experimental.pallas import tpu as pltpu
from jax.sharding import Mesh
from jax.sharding import PartitionSpec as P

AXES = ("leaf", "z_lo", "core", "z_hi", "y")
COL = ("z_hi", "y")
NX, NL, NH, NY = 4, 4, 2, 4
NZ = NL * NH
F32 = jnp.float32
HBM = pl.BlockSpec(memory_space=pltpu.HBM)
SMEM = pl.BlockSpec(memory_space=pltpu.SMEM)
VMEM = pl.BlockSpec(memory_space=pltpu.VMEM)
PARAMS = pltpu.CompilerParams(vmem_limit_bytes=56 << 20)


def way(core):
    return 1 if core == 0 else -1


def z_step(block):
    def place(z, core):
        return ((z % NL) * 2 + core) * NH + z // NL

    pairs = [(place(z, core), place((z + way(core)) % NZ, core)) for z in range(NZ) for core in range(2)]
    return lax.ppermute(block, ("z_lo", "core", "z_hi"), pairs)


def y_step(block):
    pairs = [(core * NY + y, core * NY + (y + way(core)) % NY) for y in range(NY) for core in range(2)]
    return lax.ppermute(block, ("core", "y"), pairs)


def x_step(block):
    pairs = [(x * 2 + core, (x + way(core)) % NX * 2 + core) for x in range(NX) for core in range(2)]
    return lax.ppermute(block, ("leaf", "core"), pairs)


def swap(block, axis):
    return lax.ppermute(block, axis, [(0, 1), (1, 0)])


def swap_both(halves):
    return [swap(half, "core") for half in halves]


def split(value):
    high = value.astype(jnp.bfloat16)
    return high, (value - high.astype(F32)).astype(jnp.bfloat16)


def product(left, right):
    left_high, left_low = split(left)
    right_high, right_low = split(right)
    dot = functools.partial(jnp.dot, preferred_element_type=F32)
    return dot(left_high, right_high) + (dot(left_high, right_low) + dot(left_low, right_high))


def cost(dots, n):
    return pl.CostEstimate(flops=6 * dots * n**3, bytes_accessed=12 * dots * n * n, transcendentals=0)


def light(n):
    return pl.CostEstimate(flops=n * n, bytes_accessed=12 * n * n, transcendentals=0)


def shaped(*shape):
    return jax.ShapeDtypeStruct(shape, F32)


class Place:
    def __init__(self, ref):
        self.x, self.zl, self.core, self.zh, self.y = (ref[i] for i in range(5))
        self.z = self.zh * NL + self.zl
        self.turn = 1 - 2 * self.core


def mask_kernel(mask, panel, top, bottom, turned):
    h = top.shape[0]
    for i, out in enumerate((top, bottom)):
        for j in range(2):
            part = panel[0, i * h : (i + 1) * h, j * h : (j + 1) * h] * mask[0, i, j].astype(F32)
            out[:, j * h : (j + 1) * h] = part
            turned[j * h : (j + 1) * h, i * h : (i + 1) * h] = part.T


def masked_block(mask, panel):
    n = panel.shape[1]
    return pl.pallas_call(
        mask_kernel,
        out_shape=(shaped(n // 2, n), shaped(n // 2, n), shaped(n, n)),
        in_specs=[SMEM, VMEM],
        out_specs=(VMEM, VMEM, VMEM),
        compiler_params=PARAMS,
        cost_estimate=light(n),
    )(mask, panel)


def turn_kernel(top, bottom, turned):
    h = top.shape[0]
    turned[:, :h] = top[...].T
    turned[:, h:] = bottom[...].T


def turned_block(halves):
    n = halves[0].shape[1]
    return pl.pallas_call(
        turn_kernel,
        out_shape=shaped(n, n),
        in_specs=[VMEM, VMEM],
        out_specs=VMEM,
        compiler_params=PARAMS,
        cost_estimate=light(n),
    )(*halves)


def near_steps(bounds):
    return bounds[1] - bounds[0]


class Step:
    def __init__(self, here, near, far, i):
        count = near_steps(near)
        self.near = i < count
        self.s = jnp.where(self.near, near[0] + i, far[0] + i - count)
        self.direct = jnp.equal(here.core == here.zh, self.near)
        from_z = jnp.bitwise_and(here.z - here.turn * self.s * jnp.where(self.direct, 1, -1), NZ - 1)
        self.block = jnp.bitwise_and(from_z, NL - 1)
        self.half = from_z // NL


class Gather:
    def __init__(self, here, near, far, refs, buffers):
        self.here, self.near, self.far = here, near, far
        self.steps = near_steps(near) + near_steps(far)
        self.near_root, self.far_roots, self.first, self.own, self.other = refs
        self.left_buffer, self.right_buffer, self.left_sems, self.right_sems = buffers

    def step(self, i):
        return Step(self.here, self.near, self.far, i)

    def start(self, i, slot):
        here, step = self.here, self.step(i)
        left, right = self.left_buffer, self.right_buffer

        def fetch_root(root, first_piece, piece_place):
            q = root.shape[2]
            for p in range(NY):
                to = left.at[slot, :, pl.ds(pl.multiple_of(piece_place(p) * q, q), q)]
                pltpu.make_async_copy(root.at[first_piece + p], to, self.left_sems.at[slot]).start()

        if near_steps(self.near):
            pl.when(step.near)(lambda: fetch_root(self.near_root, step.block * NY, lambda p: p))
        if near_steps(self.far):
            arrival = jnp.bitwise_and(here.turn * (here.x - step.block), NX - 1)
            for t, root in enumerate(self.far_roots):

                @pl.when(jnp.logical_and(jnp.logical_not(step.near), arrival == t))
                def _():
                    fetch_root(root, 0, lambda p: jnp.bitwise_and(here.y - here.turn * p, NY - 1))

        h = right.shape[1] // 2
        for k in range(len(self.own)):
            for ring, wanted in ((self.own, step.direct), (self.other, jnp.logical_not(step.direct))):

                @pl.when(jnp.logical_and(step.s == self.first + k, wanted))
                def _():
                    for b in range(2):
                        to = right.at[slot, pl.ds(b * h, h)]
                        pltpu.make_async_copy(ring[k][b], to, self.right_sems.at[slot]).start()

    def run(self, total):
        @pl.loop(0, self.steps)
        def _(i):
            slot = lax.rem(i, 2)

            @pl.when(i + 1 < self.steps)
            def _():
                self.start(i + 1, 1 - slot)

            for buffer, sems in ((self.left_buffer, self.left_sems), (self.right_buffer, self.right_sems)):
                pltpu.make_async_copy(buffer.at[slot], buffer.at[slot], sems.at[slot]).wait()
            half = self.step(i).half
            total[half] = total[half] + product(self.left_buffer[slot], self.right_buffer[slot])


class Pair:
    def __init__(self, here, left, buffer, sems):
        self.here, self.left, self.buffer, self.sems = here, left, buffer, sems

    def target(self, d, k):
        here = self.here
        sign = 2 * k - 1
        to_z = jnp.bitwise_and(here.z + here.turn * sign * d, NZ - 1)
        return jnp.bitwise_and(to_z, NL - 1) * 2 + jnp.where(k == 1, here.core, 1 - here.core), to_z // NL

    def start(self, d):
        here = self.here
        for k in range(2):
            block, _ = self.target(d, k)
            step = jnp.bitwise_and(here.turn * (here.y - jnp.bitwise_and(block, NY - 1)), NY - 1)
            index = jnp.where(block // NY == here.zh, step, step + NY)
            for i, ref in enumerate(self.left):

                @pl.when(index == i)
                def _():
                    pltpu.make_async_copy(ref, self.buffer.at[k], self.sems.at[k]).start()

    def run(self, d, out, right_of):
        @pl.loop(0, 2)
        def _(k):
            pltpu.make_async_copy(self.buffer.at[k], self.buffer.at[k], self.sems.at[k]).wait()
            out[k] = product(self.buffer[k], right_of(k, self.target(d, k)[1]))


def unpack(refs, sizes):
    parts = []
    for size in sizes:
        parts.append(refs[:size])
        refs = refs[size:]
    return parts + [refs]


def twos(refs):
    return [refs[i : i + 2] for i in range(0, len(refs), 2)]


def gather_kernel(near, far, first, count, fresh, d, rows, place, *refs):
    near_root, far_roots, own, other, before, left, rest = unpack(
        refs, (1 if near_steps(near) else 0, NX if near_steps(far) else 0, 2 * count, 2 * count, 0 if fresh else 1, rows)
    )
    here = Place(place)
    after, rest = rest[0], rest[1:]
    if rows:
        out, rest = rest[0], rest[1:]
    left_buffer, right_buffer, total, left_sems, right_sems, sem = rest[:6]
    near_root = near_root[0] if near_root else None
    gather = Gather(
        here,
        near,
        far,
        (near_root, far_roots, first, twos(own), twos(other)),
        (left_buffer, right_buffer, left_sems, right_sems),
    )
    gather.start(0, 0)
    if rows:
        pair = Pair(here, left, *rest[6:])
        pair.start(d)
    if fresh:
        total[...] = jnp.zeros_like(total)
    else:
        load = pltpu.make_async_copy(before[0], total, sem)
        load.start()
        load.wait()
    gather.run(total)
    store = pltpu.make_async_copy(total, after, sem)
    store.start()
    if rows:
        pair.run(d, out, lambda k, half: total[half])
    store.wait()


def accumulate(place, near, far, near_root, far_roots, ring, other, total, d=None, rows=()):
    n = ring[0][0].shape[1]
    fresh = total is None
    bounds = [b for b in (near, far) if near_steps(b)]
    first, end = min(b[0] for b in bounds), max(b[1] for b in bounds)
    roots = ([near_root] if near_steps(near) else []) + (far_roots if near_steps(far) else [])
    blocks = [half for steps in (ring, other) for block in steps[first:end] for half in block]
    operands = [place, *roots, *blocks] + ([] if fresh else [total])
    aliases = {} if fresh else {len(operands) - 1: 0}
    operands += rows
    block = pltpu.VMEM((2, n, n), F32)
    pair = pltpu.SemaphoreType.DMA((2,))
    dots = near_steps(near) + near_steps(far) + (2 if rows else 0)
    return pl.pallas_call(
        functools.partial(gather_kernel, near, far, first, end - first, fresh, d, len(rows)),
        out_shape=(shaped(2, n, n), shaped(2, n, n)) if rows else shaped(2, n, n),
        in_specs=[SMEM] + [HBM] * (len(operands) - 1),
        out_specs=(HBM, VMEM) if rows else HBM,
        scratch_shapes=[block, block, block, pair, pair, pltpu.SemaphoreType.DMA] + ([block, pair] if rows else []),
        input_output_aliases=aliases,
        compiler_params=PARAMS,
        cost_estimate=cost(dots, n),
    )(*operands)


def pair_kernel(d, place, *refs):
    left, (right, out, buffer, right_buffer, sems, right_sems) = refs[: 2 * NY], refs[2 * NY :]
    pair = Pair(Place(place), left, buffer, sems)
    pair.start(d)
    for k in range(2):
        pltpu.make_async_copy(right.at[pair.target(d, k)[1]], right_buffer.at[k], right_sems.at[k]).start()

    def right_of(k, half):
        pltpu.make_async_copy(right_buffer.at[k], right_buffer.at[k], right_sems.at[k]).wait()
        return right_buffer[k]

    pair.run(d, out, right_of)


def partial_pair(place, d, left, right):
    n = left[0].shape[0]
    block = pltpu.VMEM((2, n, n), F32)
    pair = pltpu.SemaphoreType.DMA((2,))
    return pl.pallas_call(
        functools.partial(pair_kernel, d),
        out_shape=shaped(2, n, n),
        in_specs=[SMEM] + [HBM] * (len(left) + 1),
        out_specs=VMEM,
        scratch_shapes=[block, block, pair, pair],
        compiler_params=PARAMS,
        cost_estimate=cost(2, n),
    )(place, *left, right)


def cross_kernel(place, mask, total, out, buffer, sem):
    here = Place(place)
    copy = pltpu.make_async_copy(total.at[here.zh], buffer, sem)
    copy.start()
    copy.wait()
    h = buffer.shape[0] // 2
    for i in range(2):
        for j in range(2):
            rows, cols = slice(i * h, (i + 1) * h), slice(j * h, (j + 1) * h)
            out[0, rows, cols] = -(buffer[rows, cols] * mask[0, i, j].astype(F32))


def cross_block(place, mask, total):
    n = total.shape[1]
    return pl.pallas_call(
        cross_kernel,
        out_shape=shaped(1, n, n),
        in_specs=[SMEM, SMEM, HBM],
        out_specs=VMEM,
        scratch_shapes=[pltpu.VMEM((n, n), F32), pltpu.SemaphoreType.DMA],
        compiler_params=PARAMS,
        cost_estimate=light(n),
    )(place, mask, total)


def per_device(root_inverse, lower_panel, panel_mask, factor_inverse):
    place = jnp.stack([lax.axis_index(name) for name in AXES]).astype(jnp.int32)
    far = swap(root_inverse, "z_hi")
    near_root = lax.all_gather(root_inverse, ("leaf", "y")).reshape(NX * NY, *root_inverse.shape)
    top, bottom, turned = masked_block(panel_mask, lower_panel)

    ring, other = [(top, bottom)], []
    rows_near, rows_far = [turned], []
    total = None
    pieces, far_roots = [], []
    for r in range(1, NZ):
        top, bottom = ring[-1]
        other.append(swap_both((top, bottom)))
        if len(rows_near) < NY:
            rows_near.append(y_step(rows_near[-1]))
        ring.append((z_step(top), z_step(bottom)))
        if r == 1:
            far, top, bottom = lax.optimization_barrier((far, *ring[1]))
            ring[1] = (top, bottom)
            pieces = [far]
            while len(pieces) < NY:
                pieces.append(y_step(pieces[-1]))
            far_roots = [jnp.stack(pieces)]
            while len(far_roots) < NX:
                far_roots.append(x_step(far_roots[-1]))
        if r == NL:
            rows_far = [turned_block(ring[NL])]
            while len(rows_far) < NY:
                rows_far.append(y_step(rows_far[-1]))
        if r == NZ - 2:
            total = accumulate(place, (0, r - 1), (0, 0), near_root, far_roots, ring, other, None)
            total, top, bottom = lax.optimization_barrier((total, *ring[r]))
            ring[r] = (top, bottom)
    other.append(swap_both(ring[-1]))
    total = accumulate(place, (NZ - 3, NZ - 1), (0, NZ - 1), near_root, far_roots, ring, other, total)

    rows = rows_near + rows_far
    last = (NZ - 1, NZ)
    total, out = accumulate(place, last, last, near_root, far_roots, ring, other, total, NL - 1, rows)
    cross = cross_block(place, panel_mask, total)
    h = out.shape[1] // 2
    reduced = None
    for d in range(NL - 1, -1, -1):
        if reduced is not None:
            out = partial_pair(place, d, rows, total)
        theirs = swap_both((out[0, :h], out[0, h:]))
        own = [a + b for a, b in zip((out[1, :h], out[1, h:]), theirs)]
        reduced = own if reduced is None else [z_step(a) + b for a, b in zip(reduced, own)]
    return cross, factor_inverse + jnp.concatenate(reduced, 0)[None]


def solution(mesh):
    split_mesh = Mesh(mesh.devices.reshape(NX, NL, 2, NH, NY), AXES)
    row = ("z_lo", "core")
    block = P("leaf", row, COL)
    return jax.shard_map(
        per_device,
        mesh=split_mesh,
        in_specs=(P(row, ("leaf",) + COL), block, block, block),
        out_specs=(block, block),
        check_vma=False,
    )
```

```python
import functools

import jax
import jax.numpy as jnp
from jax import lax
from jax.experimental import pallas as pl
from jax.experimental.pallas import tpu as pltpu
from jax.sharding import Mesh
from jax.sharding import PartitionSpec as P

AXES = ("leaf", "z_lo", "core", "z_hi", "y")
COL = ("z_hi", "y")
NX, NL, NH, NY = 4, 4, 2, 4
NZ = NL * NH
F32 = jnp.float32
HAVE = {5: (3, 0, 5), 6: (4, 2, 6)}
HBM = pl.BlockSpec(memory_space=pltpu.HBM)
SMEM = pl.BlockSpec(memory_space=pltpu.SMEM)
VMEM = pl.BlockSpec(memory_space=pltpu.VMEM)
PARAMS = pltpu.CompilerParams(vmem_limit_bytes=56 << 20)


def way(core):
    return 1 if core == 0 else -1


def z_step(block):
    def place(z, core):
        return ((z % NL) * 2 + core) * NH + z // NL

    pairs = [(place(z, core), place((z + way(core)) % NZ, core)) for z in range(NZ) for core in range(2)]
    return lax.ppermute(block, ("z_lo", "core", "z_hi"), pairs)


def y_step(block):
    pairs = [(core * NY + y, core * NY + (y + way(core)) % NY) for y in range(NY) for core in range(2)]
    return lax.ppermute(block, ("core", "y"), pairs)


def x_step(block):
    pairs = [(x * 2 + core, (x + way(core)) % NX * 2 + core) for x in range(NX) for core in range(2)]
    return lax.ppermute(block, ("leaf", "core"), pairs)


def swap(block, axis):
    return lax.ppermute(block, axis, [(0, 1), (1, 0)])


def swap_both(halves):
    return [swap(half, "core") for half in halves]


def split(value):
    high = value.astype(jnp.bfloat16)
    return high, (value - high.astype(F32)).astype(jnp.bfloat16)


def product(left, right):
    left_high, left_low = split(left)
    right_high, right_low = split(right)
    dot = functools.partial(jnp.dot, preferred_element_type=F32)
    return dot(left_high, right_high) + (dot(left_high, right_low) + dot(left_low, right_high))


def cost(dots, n):
    return pl.CostEstimate(flops=6 * dots * n**3, bytes_accessed=12 * dots * n * n, transcendentals=0)


def light(n):
    return pl.CostEstimate(flops=n * n, bytes_accessed=12 * n * n, transcendentals=0)


def shaped(*shape):
    return jax.ShapeDtypeStruct(shape, F32)


class Place:
    def __init__(self, ref):
        self.x, self.zl, self.core, self.zh, self.y = (ref[i] for i in range(5))
        self.z = self.zh * NL + self.zl
        self.turn = 1 - 2 * self.core


def mask_kernel(mask, panel, top, bottom, turned):
    h = top.shape[0]
    for i, out in enumerate((top, bottom)):
        for j in range(2):
            part = panel[0, i * h : (i + 1) * h, j * h : (j + 1) * h] * mask[0, i, j].astype(F32)
            out[:, j * h : (j + 1) * h] = part
            turned[j * h : (j + 1) * h, i * h : (i + 1) * h] = part.T


def masked_block(mask, panel):
    n = panel.shape[1]
    return pl.pallas_call(
        mask_kernel,
        out_shape=(shaped(n // 2, n), shaped(n // 2, n), shaped(n, n)),
        in_specs=[SMEM, VMEM],
        out_specs=(VMEM, VMEM, VMEM),
        compiler_params=PARAMS,
        cost_estimate=light(n),
    )(mask, panel)


def turn_kernel(top, bottom, turned):
    h = top.shape[0]
    turned[:, :h] = top[...].T
    turned[:, h:] = bottom[...].T


def turned_block(halves):
    n = halves[0].shape[1]
    return pl.pallas_call(
        turn_kernel,
        out_shape=shaped(n, n),
        in_specs=[VMEM, VMEM],
        out_specs=VMEM,
        compiler_params=PARAMS,
        cost_estimate=light(n),
    )(*halves)


class Step:
    def __init__(self, here, have, had, i):
        steps = have[2]
        self.far = i >= steps
        self.s = lax.rem(i, steps)
        self.direct = jnp.not_equal(here.core == here.zh, self.far)
        from_z = jnp.bitwise_and(here.z - here.turn * self.s * jnp.where(self.direct, 1, -1), NZ - 1)
        self.half = from_z // NL
        self.arrival = jnp.bitwise_and(here.turn * (here.x - from_z), NX - 1)
        now = self.arrival < jnp.where(self.far, have[1], have[0])
        before = jnp.logical_and(self.arrival < jnp.where(self.far, had[1], had[0]), self.s < had[2])
        self.ready = jnp.logical_and(now, jnp.logical_not(before))


class Gather:
    def __init__(self, here, have, had, refs, buffers):
        self.here, self.have, self.had = here, have, had
        self.near_roots, self.far_roots, self.own, self.other = refs
        self.left_buffer, self.right_buffer, self.left_sems, self.right_sems = buffers

    def step(self, i):
        return Step(self.here, self.have, self.had, i)

    def start(self, i, slot):
        here, step = self.here, self.step(i)
        left, right = self.left_buffer, self.right_buffer
        h = right.shape[1] // 2

        @pl.when(step.ready)
        def _():
            for roots, of_far in ((self.near_roots, False), (self.far_roots, True)):
                for t, root in enumerate(roots):

                    @pl.when(jnp.logical_and(step.far == of_far, step.arrival == t))
                    def _():
                        q = root.shape[2]
                        for p in range(NY):
                            at = pl.multiple_of(jnp.bitwise_and(here.y - here.turn * p, NY - 1) * q, q)
                            to = left.at[slot, :, pl.ds(at, q)]
                            pltpu.make_async_copy(root.at[p], to, self.left_sems.at[slot]).start()

            for k in range(len(self.own)):
                for ring, wanted in ((self.own, step.direct), (self.other, jnp.logical_not(step.direct))):

                    @pl.when(jnp.logical_and(step.s == k, wanted))
                    def _():
                        for b in range(2):
                            to = right.at[slot, pl.ds(b * h, h)]
                            pltpu.make_async_copy(ring[k][b], to, self.right_sems.at[slot]).start()

    def run(self, total):
        steps = 2 * self.have[2]

        @pl.loop(0, steps)
        def _(i):
            slot = lax.rem(i, 2)

            @pl.when(i + 1 < steps)
            def _():
                self.start(i + 1, 1 - slot)

            step = self.step(i)

            @pl.when(step.ready)
            def _():
                for buffer, sems in ((self.left_buffer, self.left_sems), (self.right_buffer, self.right_sems)):
                    pltpu.make_async_copy(buffer.at[slot], buffer.at[slot], sems.at[slot]).wait()
                total[step.half] = total[step.half] + product(self.left_buffer[slot], self.right_buffer[slot])


class Pair:
    def __init__(self, here, left, buffer, sems):
        self.here, self.left, self.buffer, self.sems = here, left, buffer, sems

    def target(self, i):
        here = self.here
        own = lax.rem(i, 2)
        to_z = jnp.bitwise_and(here.z + here.turn * (2 * own - 1) * (i // 2), NZ - 1)
        return jnp.bitwise_and(to_z, NL - 1) * 2 + jnp.where(own == 1, here.core, 1 - here.core), to_z // NL

    def start(self, i):
        here = self.here
        block, _ = self.target(i)
        step = jnp.bitwise_and(here.turn * (here.y - jnp.bitwise_and(block, NY - 1)), NY - 1)
        index = jnp.where(block // NY == here.zh, step, step + NY)
        slot = lax.rem(i, 2)
        for k, ref in enumerate(self.left):

            @pl.when(index == k)
            def _():
                pltpu.make_async_copy(ref, self.buffer.at[slot], self.sems.at[slot]).start()

    def run(self, order, outs, total):
        first, last = 2 * order[0], 2 * order[-1]

        @pl.loop(0, 2 * len(order))
        def _(k):
            i = first - k // 2 * 2 + lax.rem(k, 2)
            slot = lax.rem(k, 2)
            pltpu.make_async_copy(self.buffer.at[slot], self.buffer.at[slot], self.sems.at[slot]).wait()
            out = product(self.buffer[slot], total[self.target(i)[1]])
            for j, (top, bottom, own) in enumerate(outs):
                h = top.shape[0]

                @pl.when(k == 2 * j)
                def _():
                    top[...] = out[:h]
                    bottom[...] = out[h:]

                @pl.when(k == 2 * j + 1)
                def _():
                    own[...] = out

            @pl.when(i - 2 >= last)
            def _():
                self.start(i - 2)


def unpack(refs, sizes):
    parts = []
    for size in sizes:
        parts.append(refs[:size])
        refs = refs[size:]
    return parts + [refs]


def groups(refs, size):
    return [refs[i : i + size] for i in range(0, len(refs), size)]


def load(source, target, sem):
    copy = pltpu.make_async_copy(source, target, sem)
    copy.start()
    copy.wait()


def gather_kernel(have, had, rows, distance, place, *refs):
    near_roots, far_roots, own, other, before, left, rest = unpack(
        refs, (have[0], have[1], 2 * have[2], 2 * have[2], 1 if had[2] else 0, rows)
    )
    here = Place(place)
    after, rest = rest[0], rest[1:]
    if rows:
        outs, rest = rest[:3], rest[3:]
    left_buffer, right_buffer, total, left_sems, right_sems, sem = rest[:6]
    gather = Gather(
        here,
        have,
        had,
        (near_roots, far_roots, groups(own, 2), groups(other, 2)),
        (left_buffer, right_buffer, left_sems, right_sems),
    )
    gather.start(0, 0)
    if rows:
        pair = Pair(here, left, *rest[6:])
        pair.start(2 * distance)
        pair.start(2 * distance + 1)
    if had[2]:
        load(before[0], total, sem)
    else:
        total[...] = jnp.zeros_like(total)
    gather.run(total)
    store = pltpu.make_async_copy(total, after, sem)
    store.start()
    if rows:
        pair.run([distance], [outs], total)
    store.wait()


def accumulate(place, have, had, near_roots, far_roots, ring, other, total, rows=(), distance=None):
    n = ring[0][0].shape[1]
    blocks = [half for steps in (ring, other) for block in steps[: have[2]] for half in block]
    operands = [place, *near_roots[: have[0]], *far_roots[: have[1]], *blocks]
    aliases = {}
    if had[2]:
        aliases = {len(operands): 0}
        operands.append(total)
    operands += rows
    block = pltpu.VMEM((2, n, n), F32)
    pair = pltpu.SemaphoreType.DMA((2,))
    pair_outs = (shaped(n // 2, n), shaped(n // 2, n), shaped(n, n)) if rows else ()
    outs = pl.pallas_call(
        functools.partial(gather_kernel, have, had, len(rows), distance),
        out_shape=(shaped(2, n, n),) + pair_outs,
        in_specs=[SMEM] + [HBM] * (len(operands) - 1),
        out_specs=(HBM,) + (VMEM,) * len(pair_outs),
        scratch_shapes=[block, block, block, pair, pair, pltpu.SemaphoreType.DMA] + ([block, pair] if rows else []),
        input_output_aliases=aliases,
        compiler_params=PARAMS,
        cost_estimate=cost(6, n),
    )(*operands)
    return outs if rows else outs[0]


def pair_kernel(order, place, *refs):
    left, (right,), outs, (buffer, total, sems, sem) = unpack(refs, (2 * NY, 1, 3 * len(order)))
    pair = Pair(Place(place), left, buffer, sems)
    pair.start(2 * order[0])
    pair.start(2 * order[0] + 1)
    load(right, total, sem)
    pair.run(order, groups(outs, 3), total)


def pairs(place, order, left, right, dots):
    n = left[0].shape[0]
    block = pltpu.VMEM((2, n, n), F32)
    outs = pl.pallas_call(
        functools.partial(pair_kernel, order),
        out_shape=(shaped(n // 2, n), shaped(n // 2, n), shaped(n, n)) * len(order),
        in_specs=[SMEM] + [HBM] * (len(left) + 1),
        out_specs=(VMEM,) * (3 * len(order)),
        scratch_shapes=[block, block, pltpu.SemaphoreType.DMA((2,)), pltpu.SemaphoreType.DMA],
        compiler_params=PARAMS,
        cost_estimate=cost(dots, n),
    )(place, *left, right)
    return groups(outs, 3)


def join_kernel(*refs):
    refs[-1][...] = sum(ref[...] for ref in refs[1:-1]) + refs[0][...]


def joined(b, own, *halves):
    h, n = halves[0].shape
    return pl.pallas_call(
        join_kernel,
        out_shape=shaped(h, n),
        grid=(1,),
        in_specs=[pl.BlockSpec((h, n), lambda i: (b, 0))] + [pl.BlockSpec((h, n), lambda i: (0, 0))] * len(halves),
        out_specs=pl.BlockSpec((h, n), lambda i: (0, 0)),
        compiler_params=PARAMS,
        cost_estimate=light(h),
    )(own, *halves)


def cross_kernel(place, mask, total, out, buffer, sem):
    here = Place(place)
    copy = pltpu.make_async_copy(total.at[here.zh], buffer, sem)
    copy.start()
    copy.wait()
    h = buffer.shape[0] // 2
    for i in range(2):
        for j in range(2):
            rows, cols = slice(i * h, (i + 1) * h), slice(j * h, (j + 1) * h)
            out[0, rows, cols] = -(buffer[rows, cols] * mask[0, i, j].astype(F32))


def cross_block(place, mask, total):
    n = total.shape[1]
    return pl.pallas_call(
        cross_kernel,
        out_shape=shaped(1, n, n),
        in_specs=[SMEM, SMEM, HBM],
        out_specs=VMEM,
        scratch_shapes=[pltpu.VMEM((n, n), F32), pltpu.SemaphoreType.DMA],
        compiler_params=PARAMS,
        cost_estimate=light(n),
    )(place, mask, total)


def around_y_then_x(part):
    pieces = [part]
    while len(pieces) < NY:
        pieces.append(y_step(pieces[-1]))
    roots = [jnp.stack(pieces)]
    while len(roots) < NX:
        roots.append(x_step(roots[-1]))
    return roots


def per_device(root_inverse, lower_panel, panel_mask, factor_inverse):
    place = jnp.stack([lax.axis_index(name) for name in AXES]).astype(jnp.int32)
    near_roots = around_y_then_x(root_inverse)
    far = swap(root_inverse, "z_hi")
    top, bottom, turned = masked_block(panel_mask, lower_panel)

    ring, other = [(top, bottom)], []
    rows_near, rows_far = [turned], []
    had, total = (0, 0, 0), None

    def gathered(have, had, total, *pair):
        return accumulate(place, have, had, near_roots, far_roots, ring, other, total, *pair)

    for r in range(1, NZ):
        top, bottom = ring[-1]
        other.append(swap_both((top, bottom)))
        if len(rows_near) < NY:
            rows_near.append(y_step(rows_near[-1]))
        ring.append((z_step(top), z_step(bottom)))
        if r == 1:
            far, *ring[1] = lax.optimization_barrier((far, *ring[1]))
            far_roots = around_y_then_x(far)
        if r == NL:
            rows_far = [turned_block(ring[NL])]
            while len(rows_far) < NY:
                rows_far.append(y_step(rows_far[-1]))
        if r in HAVE:
            total = gathered(HAVE[r], had, total)
            had = HAVE[r]
            total, *ring[r] = lax.optimization_barrier((total, *ring[r]))
    other.append(swap_both(ring[-1]))

    rows = rows_near + rows_far
    total, *out = gathered((NX, NX, NZ), had, total, rows, NL - 1)
    cross = cross_block(place, panel_mask, total)
    outs = [out] + pairs(place, [NL - 2], rows, total, 2)
    moving = [joined(b, outs[0][2], swap(outs[0][b], "core")) for b in range(2)]
    moving, total = lax.optimization_barrier((moving, total))
    moving = [z_step(half) for half in moving]
    outs += pairs(place, list(range(NL - 3, -1, -1)), rows, total, 0)
    for out in outs[1:-1]:
        moving = [z_step(joined(b, out[2], swap(out[b], "core"), moving[b])) for b in range(2)]
    top, bottom, own = outs[-1]
    rest = jnp.concatenate([a + swap(b, "core") for a, b in zip(moving, (top, bottom))], 0)
    return cross, factor_inverse + (own + rest)[None]


def solution(mesh):
    split_mesh = Mesh(mesh.devices.reshape(NX, NL, 2, NH, NY), AXES)
    row = ("z_lo", "core")
    block = P("leaf", row, COL)
    return jax.shard_map(
        per_device,
        mesh=split_mesh,
        in_specs=(P(row, ("leaf",) + COL), block, block, block),
        out_specs=(block, block),
        check_vma=False,
    )
```

```python
import functools

import jax
import jax.numpy as jnp
from jax import lax
from jax.experimental import pallas as pl
from jax.experimental.pallas import tpu as pltpu
from jax.sharding import Mesh
from jax.sharding import PartitionSpec as P

AXES = ("leaf", "z_lo", "core", "z_hi", "y")
COL = ("z_hi", "y")
NX, NL, NH, NY = 4, 4, 2, 4
NZ = NL * NH
F32 = jnp.float32
HAVE = {4: (4, 0, 3), 6: (4, 3, 5), 7: (4, 4, 6)}
HBM = pl.BlockSpec(memory_space=pltpu.HBM)
SMEM = pl.BlockSpec(memory_space=pltpu.SMEM)
VMEM = pl.BlockSpec(memory_space=pltpu.VMEM)
PARAMS = pltpu.CompilerParams(vmem_limit_bytes=56 << 20)
SMALL = pltpu.CompilerParams(vmem_limit_bytes=16 << 20)


def way(core):
    return 1 if core == 0 else -1


def z_step(block):
    def place(z, core):
        return ((z % NL) * 2 + core) * NH + z // NL

    pairs = [(place(z, core), place((z + way(core)) % NZ, core)) for z in range(NZ) for core in range(2)]
    return lax.ppermute(block, ("z_lo", "core", "z_hi"), pairs)


def y_step(block):
    pairs = [(core * NY + y, core * NY + (y + way(core)) % NY) for y in range(NY) for core in range(2)]
    return lax.ppermute(block, ("core", "y"), pairs)


def x_step(block):
    pairs = [(x * 2 + core, (x + way(core)) % NX * 2 + core) for x in range(NX) for core in range(2)]
    return lax.ppermute(block, ("leaf", "core"), pairs)


def swap(block, axis):
    return lax.ppermute(block, axis, [(0, 1), (1, 0)])


def swap_both(halves):
    return [swap(half, "core") for half in halves]


def split(value):
    high = value.astype(jnp.bfloat16)
    return high, (value - high.astype(F32)).astype(jnp.bfloat16)


def product(left, right):
    left_high, left_low = split(left)
    right_high, right_low = split(right)
    dot = functools.partial(jnp.dot, preferred_element_type=F32)
    return dot(left_high, right_high) + (dot(left_high, right_low) + dot(left_low, right_high))


def cost(dots, n):
    return pl.CostEstimate(flops=6 * dots * n**3, bytes_accessed=12 * dots * n * n, transcendentals=0)


def light(n):
    return pl.CostEstimate(flops=n * n, bytes_accessed=12 * n * n, transcendentals=0)


def shaped(*shape):
    return jax.ShapeDtypeStruct(shape, F32)


class Place:
    def __init__(self, ref):
        self.x, self.zl, self.core, self.zh, self.y = (ref[i] for i in range(5))
        self.z = self.zh * NL + self.zl
        self.turn = 1 - 2 * self.core


def mask_kernel(mask, panel, top, bottom, turned):
    h = top.shape[0]
    for i, out in enumerate((top, bottom)):
        for j in range(2):
            part = panel[0, i * h : (i + 1) * h, j * h : (j + 1) * h] * mask[0, i, j].astype(F32)
            out[:, j * h : (j + 1) * h] = part
            turned[j * h : (j + 1) * h, i * h : (i + 1) * h] = part.T


def masked_block(mask, panel):
    n = panel.shape[1]
    return pl.pallas_call(
        mask_kernel,
        out_shape=(shaped(n // 2, n), shaped(n // 2, n), shaped(n, n)),
        in_specs=[SMEM, VMEM],
        out_specs=(VMEM, VMEM, VMEM),
        compiler_params=SMALL,
        cost_estimate=light(n),
    )(mask, panel)


def turn_kernel(top, bottom, turned):
    h = top.shape[0]
    turned[:, :h] = top[...].T
    turned[:, h:] = bottom[...].T


def turned_block(halves):
    n = halves[0].shape[1]
    return pl.pallas_call(
        turn_kernel,
        out_shape=shaped(n, n),
        in_specs=[VMEM, VMEM],
        out_specs=VMEM,
        compiler_params=SMALL,
        cost_estimate=light(n),
    )(*halves)


class Step:
    def __init__(self, here, have, had, i):
        steps = have[2]
        self.far = i >= steps
        self.s = lax.rem(i, steps)
        self.direct = jnp.not_equal(here.core == here.zh, self.far)
        from_z = jnp.bitwise_and(here.z - here.turn * self.s * jnp.where(self.direct, 1, -1), NZ - 1)
        self.half = from_z // NL
        self.arrival = jnp.bitwise_and(here.turn * (here.x - from_z), NX - 1)
        now = self.arrival < jnp.where(self.far, have[1], have[0])
        before = jnp.logical_and(self.arrival < jnp.where(self.far, had[1], had[0]), self.s < had[2])
        self.ready = jnp.logical_and(now, jnp.logical_not(before))


class Gather:
    def __init__(self, here, have, had, refs, buffers):
        self.here, self.have, self.had = here, have, had
        self.near_roots, self.far_roots, self.own, self.other = refs
        self.left_buffer, self.right_buffer, self.left_sems, self.right_sems = buffers

    def step(self, i):
        return Step(self.here, self.have, self.had, i)

    def start(self, i, slot):
        here, step = self.here, self.step(i)
        left, right = self.left_buffer, self.right_buffer
        h = right.shape[1] // 2

        @pl.when(step.ready)
        def _():
            for roots, of_far in ((self.near_roots, False), (self.far_roots, True)):
                for t, root in enumerate(roots):

                    @pl.when(jnp.logical_and(step.far == of_far, step.arrival == t))
                    def _():
                        q = root.shape[2]
                        for p in range(NY):
                            at = pl.multiple_of(jnp.bitwise_and(here.y - p, NY - 1) * q, q)
                            to = left.at[slot, :, pl.ds(at, q)]
                            pltpu.make_async_copy(root.at[p], to, self.left_sems.at[slot]).start()

            for k in range(len(self.own)):
                for ring, wanted in ((self.own, step.direct), (self.other, jnp.logical_not(step.direct))):

                    @pl.when(jnp.logical_and(step.s == k, wanted))
                    def _():
                        for b in range(2):
                            to = right.at[slot, pl.ds(b * h, h)]
                            pltpu.make_async_copy(ring[k][b], to, self.right_sems.at[slot]).start()

    def run(self, total):
        steps = 2 * self.have[2]

        @pl.loop(0, steps)
        def _(i):
            slot = lax.rem(i, 2)

            @pl.when(i + 1 < steps)
            def _():
                self.start(i + 1, 1 - slot)

            step = self.step(i)

            @pl.when(step.ready)
            def _():
                for buffer, sems in ((self.left_buffer, self.left_sems), (self.right_buffer, self.right_sems)):
                    pltpu.make_async_copy(buffer.at[slot], buffer.at[slot], sems.at[slot]).wait()
                total[step.half] = total[step.half] + product(self.left_buffer[slot], self.right_buffer[slot])


class Pair:
    def __init__(self, here, left, buffer, sems):
        self.here, self.left, self.buffer, self.sems = here, left, buffer, sems

    def target(self, i):
        here = self.here
        own = lax.rem(i, 2)
        to_z = jnp.bitwise_and(here.z + here.turn * (2 * own - 1) * (i // 2), NZ - 1)
        return jnp.bitwise_and(to_z, NL - 1) * 2 + jnp.where(own == 1, here.core, 1 - here.core), to_z // NL

    def start(self, i):
        here = self.here
        block, _ = self.target(i)
        step = jnp.bitwise_and(here.turn * (here.y - jnp.bitwise_and(block, NY - 1)), NY - 1)
        index = jnp.where(block // NY == here.zh, step, step + NY)
        slot = lax.rem(i, 2)
        for k, ref in enumerate(self.left):

            @pl.when(index == k)
            def _():
                pltpu.make_async_copy(ref, self.buffer.at[slot], self.sems.at[slot]).start()

    def run(self, order, outs, total):
        first, last = 2 * order[0], 2 * order[-1]

        @pl.loop(0, 2 * len(order))
        def _(k):
            i = first - k // 2 * 2 + lax.rem(k, 2)
            slot = lax.rem(k, 2)
            pltpu.make_async_copy(self.buffer.at[slot], self.buffer.at[slot], self.sems.at[slot]).wait()
            out = product(self.buffer[slot], total[self.target(i)[1]])
            for j, (top, bottom) in enumerate(outs):
                h = top.shape[0]

                @pl.when(k == j)
                def _():
                    top[...] = out[:h]
                    bottom[...] = out[h:]

            @pl.when(i - 2 >= last)
            def _():
                self.start(i - 2)


def unpack(refs, sizes):
    parts = []
    for size in sizes:
        parts.append(refs[:size])
        refs = refs[size:]
    return parts + [refs]


def groups(refs, size):
    return [refs[i : i + size] for i in range(0, len(refs), size)]


def load(source, target, sem):
    copy = pltpu.make_async_copy(source, target, sem)
    copy.start()
    copy.wait()


def gather_kernel(have, had, rows, distance, place, *refs):
    near_roots, far_roots, own, other, before, left, rest = unpack(
        refs, (have[0], have[1], 2 * have[2], 2 * have[2], 1 if had[2] else 0, rows)
    )
    here = Place(place)
    after, rest = rest[0], rest[1:]
    if rows:
        outs, rest = groups(rest[:4], 2), rest[4:]
    left_buffer, right_buffer, total, left_sems, right_sems, sem = rest[:6]
    gather = Gather(
        here,
        have,
        had,
        (near_roots, far_roots, groups(own, 2), groups(other, 2)),
        (left_buffer, right_buffer, left_sems, right_sems),
    )
    gather.start(0, 0)
    if rows:
        pair = Pair(here, left, *rest[6:])
        pair.start(2 * distance)
        pair.start(2 * distance + 1)
    if had[2]:
        load(before[0], total, sem)
    else:
        total[...] = jnp.zeros_like(total)
    gather.run(total)
    store = pltpu.make_async_copy(total, after, sem)
    store.start()
    if rows:
        pair.run([distance], outs, total)
    store.wait()


def accumulate(place, have, had, near_roots, far_roots, ring, other, total, rows=(), distance=None):
    n = ring[0][0].shape[1]
    blocks = [half for steps in (ring, other) for block in steps[: have[2]] for half in block]
    operands = [place, *near_roots[: have[0]], *far_roots[: have[1]], *blocks]
    aliases = {}
    if had[2]:
        aliases = {len(operands): 0}
        operands.append(total)
    operands += rows
    block = pltpu.VMEM((2, n, n), F32)
    pair = pltpu.SemaphoreType.DMA((2,))
    pair_outs = (shaped(n // 2, n),) * 4 if rows else ()
    outs = pl.pallas_call(
        functools.partial(gather_kernel, have, had, len(rows), distance),
        out_shape=(shaped(2, n, n),) + pair_outs,
        in_specs=[SMEM] + [HBM] * (len(operands) - 1),
        out_specs=(HBM,) + (VMEM,) * len(pair_outs),
        scratch_shapes=[block, block, block, pair, pair, pltpu.SemaphoreType.DMA] + ([block, pair] if rows else []),
        input_output_aliases=aliases,
        compiler_params=PARAMS,
        cost_estimate=cost(6, n),
    )(*operands)
    return outs if rows else outs[0]


def pair_kernel(order, place, *refs):
    left, (right,), outs, (buffer, total, sems, sem) = unpack(refs, (2 * NY, 1, 4 * len(order)))
    pair = Pair(Place(place), left, buffer, sems)
    pair.start(2 * order[0])
    pair.start(2 * order[0] + 1)
    load(right, total, sem)
    pair.run(order, groups(outs, 2), total)


def pairs(place, order, left, right, dots):
    n = left[0].shape[0]
    block = pltpu.VMEM((2, n, n), F32)
    outs = pl.pallas_call(
        functools.partial(pair_kernel, order),
        out_shape=(shaped(n // 2, n),) * (4 * len(order)),
        in_specs=[SMEM] + [HBM] * (len(left) + 1),
        out_specs=(VMEM,) * (4 * len(order)),
        scratch_shapes=[block, block, pltpu.SemaphoreType.DMA((2,)), pltpu.SemaphoreType.DMA],
        compiler_params=PARAMS,
        cost_estimate=cost(dots, n),
    )(place, *left, right)
    return groups(outs, 4)


def cross_kernel(place, mask, total, out, buffer, sem):
    here = Place(place)
    copy = pltpu.make_async_copy(total.at[here.zh], buffer, sem)
    copy.start()
    copy.wait()
    h = buffer.shape[0] // 2
    for i in range(2):
        for j in range(2):
            rows, cols = slice(i * h, (i + 1) * h), slice(j * h, (j + 1) * h)
            out[0, rows, cols] = -(buffer[rows, cols] * mask[0, i, j].astype(F32))


def cross_block(place, mask, total):
    n = total.shape[1]
    return pl.pallas_call(
        cross_kernel,
        out_shape=shaped(1, n, n),
        in_specs=[SMEM, SMEM, HBM],
        out_specs=VMEM,
        scratch_shapes=[pltpu.VMEM((n, n), F32), pltpu.SemaphoreType.DMA],
        compiler_params=SMALL,
        cost_estimate=light(n),
    )(place, mask, total)


def from_all_y(part):
    moved = [lax.ppermute(part, "y", [(y, (y + k) % NY) for y in range(NY)]) for k in range(1, NY)]
    return jnp.stack([part] + moved)


def per_device(root_inverse, lower_panel, panel_mask, factor_inverse):
    place = jnp.stack([lax.axis_index(name) for name in AXES]).astype(jnp.int32)
    near_roots, far_roots = [from_all_y(root_inverse)], []
    far = swap(root_inverse, "z_hi")
    top, bottom, turned = masked_block(panel_mask, lower_panel)

    ring, other = [(top, bottom)], []
    rows_near, rows_far = [turned], []
    had, total = (0, 0, 0), None
    for r in range(1, NZ):
        top, bottom = ring[-1]
        other.append(swap_both((top, bottom)))
        ring.append([z_step(top), z_step(bottom)])
        if r == 2:
            far_roots.append(from_all_y(far))
            y_rows = None
        else:
            y_rows = rows_near if r < NL + 1 else rows_far
            y_rows.append(y_step(y_rows[-1]))
        x_roots = near_roots if r < NX else far_roots
        if r < 2 * NX - 1:
            x_roots.append(x_step(x_roots[-1]))
        if r in HAVE:
            total = accumulate(place, HAVE[r], had, near_roots, far_roots, ring, other, total)
            had = HAVE[r]
        round_ends = [(ring[r], 1)] + ([(y_rows, -1)] if y_rows else []) + ([(x_roots, -1)] if r < 2 * NX - 1 else [])
        values = [into[at] for into, at in round_ends]
        if r == 1:
            ring[1][0], far, *values = lax.optimization_barrier((ring[1][0], far, *values))
        elif r in HAVE:
            total, *values = lax.optimization_barrier((total, *values))
        else:
            values = lax.optimization_barrier(values)
        for (into, at), value in zip(round_ends, values):
            into[at] = value
        if r == NL:
            rows_far = [turned_block(ring[NL])]
    other.append(swap_both(ring[-1]))

    rows = rows_near + rows_far
    have = (NX, NX, NZ)
    total, *out = accumulate(place, have, had, near_roots, far_roots, ring, other, total, rows, NL - 1)
    cross = cross_block(place, panel_mask, total)
    moving = [z_step(own + theirs) for own, theirs in zip(out[2:], swap_both(out[:2]))]
    outs = pairs(place, list(range(NL - 2, -1, -1)), rows, total, 0)
    for out in outs[:-1]:
        moving = [z_step(a + own + theirs) for a, own, theirs in zip(moving, out[2:], swap_both(out[:2]))]
    out = outs[-1]
    rest = [a + own + theirs for a, own, theirs in zip(moving, out[2:], swap_both(out[:2]))]
    return cross, factor_inverse + jnp.concatenate(rest, 0)[None]


def solution(mesh):
    split_mesh = Mesh(mesh.devices.reshape(NX, NL, 2, NH, NY), AXES)
    row = ("z_lo", "core")
    block = P("leaf", row, COL)
    return jax.shard_map(
        per_device,
        mesh=split_mesh,
        in_specs=(P(row, ("leaf",) + COL), block, block, block),
        out_specs=(block, block),
        check_vma=False,
    )
```

```python
import functools

import jax
import jax.numpy as jnp
from jax import lax
from jax.experimental import pallas as pl
from jax.experimental.pallas import tpu as pltpu
from jax.sharding import Mesh
from jax.sharding import PartitionSpec as P

AXES = ("leaf", "z_lo", "core", "z_hi", "y")
COL = ("z_hi", "y")
NX, NL, NH, NY = 4, 4, 2, 4
NZ = NL * NH
F32 = jnp.float32
HAVE = {5: (2, 5), 7: (3, 7)}
HBM = pl.BlockSpec(memory_space=pltpu.HBM)
SMEM = pl.BlockSpec(memory_space=pltpu.SMEM)
VMEM = pl.BlockSpec(memory_space=pltpu.VMEM)
PARAMS = pltpu.CompilerParams(vmem_limit_bytes=56 << 20)
SMALL = pltpu.CompilerParams(vmem_limit_bytes=16 << 20)


def way(core):
    return 1 if core == 0 else -1


def z_step(block):
    def place(z, core):
        return ((z % NL) * 2 + core) * NH + z // NL

    pairs = [(place(z, core), place((z + way(core)) % NZ, core)) for z in range(NZ) for core in range(2)]
    return lax.ppermute(block, ("z_lo", "core", "z_hi"), pairs)


def y_step(block):
    pairs = [(core * NY + y, core * NY + (y + way(core)) % NY) for y in range(NY) for core in range(2)]
    return lax.ppermute(block, ("core", "y"), pairs)


def x_step(block):
    pairs = [(x * 2 + core, (x + way(core)) % NX * 2 + core) for x in range(NX) for core in range(2)]
    return lax.ppermute(block, ("leaf", "core"), pairs)


def swap(block, axis):
    return lax.ppermute(block, axis, [(0, 1), (1, 0)])


def swap_both(halves):
    return [swap(half, "core") for half in halves]


def split(value):
    high = value.astype(jnp.bfloat16)
    return high, (value - high.astype(F32)).astype(jnp.bfloat16)


def products(lefts, right):
    dot = functools.partial(jnp.dot, preferred_element_type=F32)
    right_high, right_low = split(right)
    outs = []
    for left in lefts:
        left_high, left_low = split(left)
        outs.append(dot(left_high, right_high) + (dot(left_high, right_low) + dot(left_low, right_high)))
    return outs


def cost(dots, n):
    return pl.CostEstimate(flops=6 * dots * n**3, bytes_accessed=12 * dots * n * n, transcendentals=0)


def light(n):
    return pl.CostEstimate(flops=n * n, bytes_accessed=12 * n * n, transcendentals=0)


def shaped(*shape):
    return jax.ShapeDtypeStruct(shape, F32)


class Place:
    def __init__(self, ref):
        self.x, self.zl, self.core, self.zh, self.y = (ref[i] for i in range(5))
        self.z = self.zh * NL + self.zl
        self.turn = 1 - 2 * self.core


def mask_kernel(mask, panel, top, bottom, turned):
    h = top.shape[0]
    for i, out in enumerate((top, bottom)):
        for j in range(2):
            part = panel[0, i * h : (i + 1) * h, j * h : (j + 1) * h] * mask[0, i, j].astype(F32)
            out[:, j * h : (j + 1) * h] = part
            turned[j * h : (j + 1) * h, i * h : (i + 1) * h] = part.T


def masked_block(mask, panel):
    n = panel.shape[1]
    return pl.pallas_call(
        mask_kernel,
        out_shape=(shaped(n // 2, n), shaped(n // 2, n), shaped(n, n)),
        in_specs=[SMEM, VMEM],
        out_specs=(VMEM, VMEM, VMEM),
        compiler_params=SMALL,
        cost_estimate=light(n),
    )(mask, panel)


def turn_kernel(top, bottom, turned):
    h = top.shape[0]
    turned[:, :h] = top[...].T
    turned[:, h:] = bottom[...].T


def turned_block(halves):
    n = halves[0].shape[1]
    return pl.pallas_call(
        turn_kernel,
        out_shape=shaped(n, n),
        in_specs=[VMEM, VMEM],
        out_specs=VMEM,
        compiler_params=SMALL,
        cost_estimate=light(n),
    )(*halves)


class Step:
    def __init__(self, here, have, had, s):
        from_z = jnp.bitwise_and(here.z - here.turn * s, NZ - 1)
        self.half = from_z // NL
        self.arrival = jnp.bitwise_and(here.turn * (here.x - from_z), NX - 1)
        before = jnp.logical_and(self.arrival < had[0], s < had[1])
        self.ready = jnp.logical_and(self.arrival < have[0], jnp.logical_not(before))


class Gather:
    def __init__(self, here, have, had, roots, ring, buffers):
        self.here, self.have, self.had, self.roots, self.ring = here, have, had, roots, ring
        self.left_buffer, self.right_buffer, self.left_sems, self.right_sems = buffers

    def step(self, s):
        return Step(self.here, self.have, self.had, s)

    def start(self, s, slot):
        here, step = self.here, self.step(s)
        left, right = self.left_buffer, self.right_buffer
        h = right.shape[1] // 2

        @pl.when(step.ready)
        def _():
            for t, pieces in enumerate(self.roots):

                @pl.when(step.arrival == t)
                def _():
                    q = pieces[0].shape[3]
                    for p in range(NY):
                        at = pl.multiple_of(jnp.bitwise_and(here.y - p, NY - 1) * q, q)
                        source, to = pieces[p // 2].at[p % 2], left.at[slot, :, :, pl.ds(at, q)]
                        pltpu.make_async_copy(source, to, self.left_sems.at[slot]).start()

            for k, halves in enumerate(self.ring):

                @pl.when(s == k)
                def _():
                    for b in range(2):
                        to = right.at[slot, pl.ds(b * h, h)]
                        pltpu.make_async_copy(halves[b], to, self.right_sems.at[slot]).start()

    def run(self, totals):
        steps = self.have[1]

        @pl.loop(0, steps)
        def _(s):
            slot = lax.rem(s, 2)

            @pl.when(s + 1 < steps)
            def _():
                self.start(s + 1, 1 - slot)

            step = self.step(s)

            @pl.when(step.ready)
            def _():
                for buffer, sems in ((self.left_buffer, self.left_sems), (self.right_buffer, self.right_sems)):
                    pltpu.make_async_copy(buffer.at[slot], buffer.at[slot], sems.at[slot]).wait()
                left = self.left_buffer
                for total, out in zip(totals, products((left[slot, 0], left[slot, 1]), self.right_buffer[slot])):
                    total[step.half] = total[step.half] + out


class Pair:
    def __init__(self, here, left, buffer, sems):
        self.here, self.left, self.buffer, self.sems = here, left, buffer, sems

    def target(self, i):
        here = self.here
        own = lax.rem(i, 2)
        to_z = jnp.bitwise_and(here.z + here.turn * (2 * own - 1) * (i // 2), NZ - 1)
        return jnp.bitwise_and(to_z, NL - 1) * 2 + jnp.where(own == 1, here.core, 1 - here.core), to_z // NL

    def start(self, i):
        here = self.here
        block, _ = self.target(i)
        step = jnp.bitwise_and(here.turn * (here.y - jnp.bitwise_and(block, NY - 1)), NY - 1)
        index = jnp.where(block // NY == here.zh, step, step + NY)
        slot = lax.rem(i, 2)
        for k, ref in enumerate(self.left):

            @pl.when(index == k)
            def _():
                pltpu.make_async_copy(ref, self.buffer.at[slot], self.sems.at[slot]).start()

    def run(self, order, outs, total):
        first, last = 2 * order[0], 2 * order[-1]

        @pl.loop(0, 2 * len(order))
        def _(k):
            i = first - k // 2 * 2 + lax.rem(k, 2)
            slot = lax.rem(k, 2)
            pltpu.make_async_copy(self.buffer.at[slot], self.buffer.at[slot], self.sems.at[slot]).wait()
            (out,) = products((self.buffer[slot],), total[self.target(i)[1]])
            for j, (top, bottom) in enumerate(outs):
                h = top.shape[0]

                @pl.when(k == j)
                def _():
                    top[...] = out[:h]
                    bottom[...] = out[h:]

            @pl.when(i - 2 >= last)
            def _():
                self.start(i - 2)


def unpack(refs, sizes):
    parts = []
    for size in sizes:
        parts.append(refs[:size])
        refs = refs[size:]
    return parts + [refs]


def groups(refs, size):
    return [refs[i : i + size] for i in range(0, len(refs), size)]


def load(source, target, sem):
    copy = pltpu.make_async_copy(source, target, sem)
    copy.start()
    copy.wait()


def gather_kernel(have, had, place, *refs):
    roots, ring, before, afters, rest = unpack(refs, (2 * have[0], 2 * have[1], 2 if had[1] else 0, 2))
    left_buffer, right_buffer, own, theirs, left_sems, right_sems, sems = rest
    totals = (own, theirs)
    buffers = (left_buffer, right_buffer, left_sems, right_sems)
    gather = Gather(Place(place), have, had, groups(roots, 2), groups(ring, 2), buffers)
    gather.start(0, 0)
    loads = [pltpu.make_async_copy(ref, total, sems.at[k]) for k, (ref, total) in enumerate(zip(before, totals))]
    for copy in loads:
        copy.start()
    for copy in loads:
        copy.wait()
    if not loads:
        for total in totals:
            total[...] = jnp.zeros_like(total)
    gather.run(totals)
    stores = [pltpu.make_async_copy(total, ref, sems.at[k]) for k, (ref, total) in enumerate(zip(afters, totals))]
    for copy in stores:
        copy.start()
    for copy in stores:
        copy.wait()


def accumulate(place, have, had, roots, ring, totals):
    n = ring[0][0].shape[1]
    operands = [place] + [part for pieces in roots[: have[0]] for part in pieces]
    operands += [half for block in ring[: have[1]] for half in block]
    aliases = {}
    if had[1]:
        aliases = {len(operands): 0, len(operands) + 1: 1}
        operands += totals
    block = pltpu.VMEM((2, n, n), F32)
    pair = pltpu.SemaphoreType.DMA((2,))
    return pl.pallas_call(
        functools.partial(gather_kernel, have, had),
        out_shape=(shaped(2, n, n),) * 2,
        in_specs=[SMEM] + [HBM] * (len(operands) - 1),
        out_specs=(HBM,) * 2,
        scratch_shapes=[pltpu.VMEM((2, 2, n, n), F32), block, block, block, pair, pair, pair],
        input_output_aliases=aliases,
        compiler_params=PARAMS,
        cost_estimate=cost(6, n),
    )(*operands)


def first_kernel(distance, place, *refs):
    left, (own, theirs, ancestor), outs, (buffer, total, extra, sems, total_sems) = unpack(refs, (2 * NY, 3, 4))
    pair = Pair(Place(place), left, buffer, sems)
    pair.start(2 * distance)
    pair.start(2 * distance + 1)
    loads = [pltpu.make_async_copy(a, b, total_sems.at[k]) for k, (a, b) in enumerate(((own, total), (theirs, extra)))]
    for copy in loads:
        copy.start()
    for copy in loads:
        copy.wait()
    total[...] = total[...] + extra[...]
    store = pltpu.make_async_copy(total, ancestor, total_sems.at[0])
    store.start()
    pair.run([distance], groups(outs, 2), total)
    store.wait()


def first_pair(place, distance, left, own, theirs):
    n = left[0].shape[0]
    block = pltpu.VMEM((2, n, n), F32)
    pair = pltpu.SemaphoreType.DMA((2,))

    def body(place, *refs):
        ins, outs = refs[: len(left) + 2], refs[len(left) + 2 :]
        first_kernel(distance, place, *ins, *outs)

    return pl.pallas_call(
        body,
        out_shape=(shaped(2, n, n),) + (shaped(n // 2, n),) * 4,
        in_specs=[SMEM] + [HBM] * (len(left) + 2),
        out_specs=(HBM,) + (VMEM,) * 4,
        scratch_shapes=[block, block, block, pair, pair],
        compiler_params=PARAMS,
        cost_estimate=cost(2, n),
    )(place, *left, own, theirs)


def pair_kernel(order, place, *refs):
    left, (right,), outs, (buffer, total, sems, sem) = unpack(refs, (2 * NY, 1, 4 * len(order)))
    pair = Pair(Place(place), left, buffer, sems)
    pair.start(2 * order[0])
    pair.start(2 * order[0] + 1)
    load(right, total, sem)
    pair.run(order, groups(outs, 2), total)


def pairs(place, order, left, right, dots):
    n = left[0].shape[0]
    block = pltpu.VMEM((2, n, n), F32)
    outs = pl.pallas_call(
        functools.partial(pair_kernel, order),
        out_shape=(shaped(n // 2, n),) * (4 * len(order)),
        in_specs=[SMEM] + [HBM] * (len(left) + 1),
        out_specs=(VMEM,) * (4 * len(order)),
        scratch_shapes=[block, block, pltpu.SemaphoreType.DMA((2,)), pltpu.SemaphoreType.DMA],
        compiler_params=PARAMS,
        cost_estimate=cost(dots, n),
    )(place, *left, right)
    return groups(outs, 4)


def cross_kernel(place, mask, total, out, buffer, sem):
    here = Place(place)
    copy = pltpu.make_async_copy(total.at[here.zh], buffer, sem)
    copy.start()
    copy.wait()
    h = buffer.shape[0] // 2
    for i in range(2):
        for j in range(2):
            rows, cols = slice(i * h, (i + 1) * h), slice(j * h, (j + 1) * h)
            out[0, rows, cols] = -(buffer[rows, cols] * mask[0, i, j].astype(F32))


def cross_block(place, mask, total):
    n = total.shape[1]
    return pl.pallas_call(
        cross_kernel,
        out_shape=shaped(1, n, n),
        in_specs=[SMEM, SMEM, HBM],
        out_specs=VMEM,
        scratch_shapes=[pltpu.VMEM((n, n), F32), pltpu.SemaphoreType.DMA],
        compiler_params=SMALL,
        cost_estimate=light(n),
    )(place, mask, total)


def from_all_y(part):
    return [part] + [lax.ppermute(part, "y", [(y, (y + k) % NY) for y in range(NY)]) for k in range(1, NY)]


def per_device(root_inverse, lower_panel, panel_mask, factor_inverse):
    place = jnp.stack([lax.axis_index(name) for name in AXES]).astype(jnp.int32)
    core, zh = lax.axis_index("core"), lax.axis_index("z_hi")
    away = swap(root_inverse, "z_hi")
    top, bottom, turned, away = lax.optimization_barrier((*masked_block(panel_mask, lower_panel), away))

    good = core == zh
    kept, sent = jnp.where(good, root_inverse, away), jnp.where(good, away, root_inverse)
    pieces = from_all_y(jnp.stack([kept, swap(sent, "core")]))
    roots = [[jnp.stack(pieces[:2]), jnp.stack(pieces[2:])]]
    while len(roots) < NX:
        roots.append([x_step(part) for part in roots[-1]])

    ring = [[top, bottom]]
    rows_near, rows_far = [turned], []
    had, totals = (0, 0), ()
    for r in range(1, NZ):
        ring.append([z_step(half) for half in ring[-1]])
        ends = [(ring[r], 1)]
        if r != 1:
            rows = rows_near if r < NL + 1 else rows_far
            rows.append(y_step(rows[-1]))
            ends.append((rows, -1))
        if r in HAVE:
            totals = list(accumulate(place, HAVE[r], had, roots, ring, totals))
            had = HAVE[r]
            ends.append((totals, 0))
        values = lax.optimization_barrier([into[at] for into, at in ends])
        for (into, at), value in zip(ends, values):
            into[at] = value
        if r == NL:
            rows_far = [turned_block(ring[NL])]
    own, theirs = accumulate(place, (NX, NZ), had, roots, ring, totals)

    rows = rows_near + rows_far
    total, *out = first_pair(place, NL - 1, rows, own, swap(theirs, "core"))
    cross = cross_block(place, panel_mask, total)
    moving = [z_step(own + theirs) for own, theirs in zip(out[2:], swap_both(out[:2]))]
    outs = pairs(place, list(range(NL - 2, -1, -1)), rows, total, 0)
    for out in outs[:-1]:
        moving = [z_step(a + own + theirs) for a, own, theirs in zip(moving, out[2:], swap_both(out[:2]))]
    out = outs[-1]
    rest = [a + own + theirs for a, own, theirs in zip(moving, out[2:], swap_both(out[:2]))]
    return cross, factor_inverse + jnp.concatenate(rest, 0)[None]


def solution(mesh):
    split_mesh = Mesh(mesh.devices.reshape(NX, NL, 2, NH, NY), AXES)
    row = ("z_lo", "core")
    block = P("leaf", row, COL)
    return jax.shard_map(
        per_device,
        mesh=split_mesh,
        in_specs=(P(row, ("leaf",) + COL), block, block, block),
        out_specs=(block, block),
        check_vma=False,
    )
```

```python
import functools

import jax
import jax.numpy as jnp
from jax import lax
from jax.experimental import pallas as pl
from jax.experimental.pallas import tpu as pltpu
from jax.sharding import Mesh
from jax.sharding import PartitionSpec as P

AXES = ("leaf", "z_lo", "core", "z_hi", "y")
COL = ("z_hi", "y")
NX, NL, NH, NY = 4, 4, 2, 4
NZ = NL * NH
F32 = jnp.float32
HAVE = {6: (2, 6), 8: (3, 8)}
HBM = pl.BlockSpec(memory_space=pltpu.HBM)
SMEM = pl.BlockSpec(memory_space=pltpu.SMEM)
VMEM = pl.BlockSpec(memory_space=pltpu.VMEM)
PARAMS = pltpu.CompilerParams(vmem_limit_bytes=56 << 20)
SMALL = pltpu.CompilerParams(vmem_limit_bytes=16 << 20)


def way(core):
    return 1 if core == 0 else -1


def z_step(block):
    def place(z, core):
        return ((z % NL) * 2 + core) * NH + z // NL

    pairs = [(place(z, core), place((z + way(core)) % NZ, core)) for z in range(NZ) for core in range(2)]
    return lax.ppermute(block, ("z_lo", "core", "z_hi"), pairs)


def y_step(block):
    pairs = [(core * NY + y, core * NY + (y + way(core)) % NY) for y in range(NY) for core in range(2)]
    return lax.ppermute(block, ("core", "y"), pairs)


def x_step(block):
    pairs = [(x * 2 + core, (x + way(core)) % NX * 2 + core) for x in range(NX) for core in range(2)]
    return lax.ppermute(block, ("leaf", "core"), pairs)


def swap(block, axis):
    return lax.ppermute(block, axis, [(0, 1), (1, 0)])


def swap_both(halves):
    return [swap(half, "core") for half in halves]


def split(value):
    high = value.astype(jnp.bfloat16)
    return high, (value - high.astype(F32)).astype(jnp.bfloat16)


def products(lefts, right):
    dot = functools.partial(jnp.dot, preferred_element_type=F32)
    right_high, right_low = split(right)
    outs = []
    for left in lefts:
        left_high, left_low = split(left)
        outs.append(dot(left_high, right_high) + (dot(left_high, right_low) + dot(left_low, right_high)))
    return outs


def cost(dots, n):
    return pl.CostEstimate(flops=6 * dots * n**3, bytes_accessed=12 * dots * n * n, transcendentals=0)


def light(n):
    return pl.CostEstimate(flops=n * n, bytes_accessed=12 * n * n, transcendentals=0)


def shaped(*shape):
    return jax.ShapeDtypeStruct(shape, F32)


class Place:
    def __init__(self, ref):
        self.x, self.zl, self.core, self.zh, self.y = (ref[i] for i in range(5))
        self.z = self.zh * NL + self.zl
        self.turn = 1 - 2 * self.core


def mask_kernel(mask, panel, out, turned):
    h = out.shape[0] // 2
    for i in range(2):
        for j in range(2):
            rows, cols = slice(i * h, (i + 1) * h), slice(j * h, (j + 1) * h)
            part = panel[0, rows, cols] * mask[0, i, j].astype(F32)
            out[rows, cols] = part
            turned[cols, rows] = part.T


def masked_block(mask, panel):
    n = panel.shape[1]
    return pl.pallas_call(
        mask_kernel,
        out_shape=(shaped(n, n), shaped(n, n)),
        in_specs=[SMEM, VMEM],
        out_specs=(VMEM, VMEM),
        compiler_params=SMALL,
        cost_estimate=light(n),
    )(mask, panel)


def turn_kernel(block, turned):
    turned[...] = block[...].T


def turned_block(block):
    n = block.shape[0]
    return pl.pallas_call(
        turn_kernel,
        out_shape=shaped(n, n),
        in_specs=[VMEM],
        out_specs=VMEM,
        compiler_params=SMALL,
        cost_estimate=light(n),
    )(block)


class Step:
    def __init__(self, here, have, had, s):
        from_z = jnp.bitwise_and(here.z - here.turn * s, NZ - 1)
        self.half = from_z // NL
        self.arrival = jnp.bitwise_and(here.turn * (here.x - from_z), NX - 1)
        before = jnp.logical_and(self.arrival < had[0], s < had[1])
        self.ready = jnp.logical_and(self.arrival < have[0], jnp.logical_not(before))


class Gather:
    def __init__(self, here, have, had, roots, ring, buffers):
        self.here, self.have, self.had, self.roots, self.ring = here, have, had, roots, ring
        self.left_buffer, self.right_buffer, self.left_sems, self.right_sems = buffers

    def step(self, s):
        return Step(self.here, self.have, self.had, s)

    def start(self, s, slot):
        here, step = self.here, self.step(s)
        left, right = self.left_buffer, self.right_buffer

        @pl.when(step.ready)
        def _():
            for t, pieces in enumerate(self.roots):

                @pl.when(step.arrival == t)
                def _():
                    q = pieces[0].shape[3]
                    for p in range(NY):
                        at = pl.multiple_of(jnp.bitwise_and(here.y - p, NY - 1) * q, q)
                        source, to = pieces[p // 2].at[p % 2], left.at[slot, :, :, pl.ds(at, q)]
                        pltpu.make_async_copy(source, to, self.left_sems.at[slot]).start()

            for k, block in enumerate(self.ring):

                @pl.when(s == k)
                def _():
                    pltpu.make_async_copy(block, right.at[slot], self.right_sems.at[slot]).start()

    def run(self, totals):
        steps = self.have[1]

        @pl.loop(0, steps)
        def _(s):
            slot = lax.rem(s, 2)

            @pl.when(s + 1 < steps)
            def _():
                self.start(s + 1, 1 - slot)

            step = self.step(s)

            @pl.when(step.ready)
            def _():
                for buffer, sems in ((self.left_buffer, self.left_sems), (self.right_buffer, self.right_sems)):
                    pltpu.make_async_copy(buffer.at[slot], buffer.at[slot], sems.at[slot]).wait()
                left = self.left_buffer
                for total, out in zip(totals, products((left[slot, 0], left[slot, 1]), self.right_buffer[slot])):
                    total[step.half] = total[step.half] + out


class Pair:
    def __init__(self, here, left, buffer, sems):
        self.here, self.left, self.buffer, self.sems = here, left, buffer, sems

    def target(self, i):
        here = self.here
        own = lax.rem(i, 2)
        to_z = jnp.bitwise_and(here.z + here.turn * (2 * own - 1) * (i // 2), NZ - 1)
        return jnp.bitwise_and(to_z, NL - 1) * 2 + jnp.where(own == 1, here.core, 1 - here.core), to_z // NL

    def start(self, i):
        here = self.here
        block, _ = self.target(i)
        step = jnp.bitwise_and(here.turn * (here.y - jnp.bitwise_and(block, NY - 1)), NY - 1)
        index = jnp.where(block // NY == here.zh, step, step + NY)
        slot = lax.rem(i, 2)
        for k, ref in enumerate(self.left):

            @pl.when(index == k)
            def _():
                pltpu.make_async_copy(ref, self.buffer.at[slot], self.sems.at[slot]).start()

    def run(self, order, outs, total):
        first, last = 2 * order[0], 2 * order[-1]

        @pl.loop(0, 2 * len(order))
        def _(k):
            i = first - k // 2 * 2 + lax.rem(k, 2)
            slot = lax.rem(k, 2)
            pltpu.make_async_copy(self.buffer.at[slot], self.buffer.at[slot], self.sems.at[slot]).wait()
            (out,) = products((self.buffer[slot],), total[self.target(i)[1]])
            for j, (top, bottom) in enumerate(outs):
                h = top.shape[0]

                @pl.when(k == j)
                def _():
                    top[...] = out[:h]
                    bottom[...] = out[h:]

            @pl.when(i - 2 >= last)
            def _():
                self.start(i - 2)


def unpack(refs, sizes):
    parts = []
    for size in sizes:
        parts.append(refs[:size])
        refs = refs[size:]
    return parts + [refs]


def groups(refs, size):
    return [refs[i : i + size] for i in range(0, len(refs), size)]


def load(source, target, sem):
    copy = pltpu.make_async_copy(source, target, sem)
    copy.start()
    copy.wait()


def gather_kernel(have, had, place, *refs):
    roots, ring, before, afters, rest = unpack(refs, (2 * have[0], have[1], 2 if had[1] else 0, 2))
    left_buffer, right_buffer, own, theirs, left_sems, right_sems, sems = rest
    totals = (own, theirs)
    buffers = (left_buffer, right_buffer, left_sems, right_sems)
    gather = Gather(Place(place), have, had, groups(roots, 2), ring, buffers)
    gather.start(0, 0)
    loads = [pltpu.make_async_copy(ref, total, sems.at[k]) for k, (ref, total) in enumerate(zip(before, totals))]
    for copy in loads:
        copy.start()
    for copy in loads:
        copy.wait()
    if not loads:
        for total in totals:
            total[...] = jnp.zeros_like(total)
    gather.run(totals)
    stores = [pltpu.make_async_copy(total, ref, sems.at[k]) for k, (ref, total) in enumerate(zip(afters, totals))]
    for copy in stores:
        copy.start()
    for copy in stores:
        copy.wait()


def accumulate(place, have, had, roots, ring, totals):
    n = ring[0].shape[0]
    operands = [place] + [part for pieces in roots[: have[0]] for part in pieces]
    operands += ring[: have[1]]
    aliases = {}
    if had[1]:
        aliases = {len(operands): 0, len(operands) + 1: 1}
        operands += totals
    block = pltpu.VMEM((2, n, n), F32)
    pair = pltpu.SemaphoreType.DMA((2,))
    return pl.pallas_call(
        functools.partial(gather_kernel, have, had),
        out_shape=(shaped(2, n, n),) * 2,
        in_specs=[SMEM] + [HBM] * (len(operands) - 1),
        out_specs=(HBM,) * 2,
        scratch_shapes=[pltpu.VMEM((2, 2, n, n), F32), block, block, block, pair, pair, pair],
        input_output_aliases=aliases,
        compiler_params=PARAMS,
        cost_estimate=cost(6, n),
    )(*operands)


def first_kernel(order, place, *refs):
    left, (own, theirs, ancestor), outs, (buffer, total, extra, sems, total_sems) = unpack(refs, (2 * NY, 3, 4 * len(order)))
    pair = Pair(Place(place), left, buffer, sems)
    pair.start(2 * order[0])
    pair.start(2 * order[0] + 1)
    loads = [pltpu.make_async_copy(a, b, total_sems.at[k]) for k, (a, b) in enumerate(((own, total), (theirs, extra)))]
    for copy in loads:
        copy.start()
    for copy in loads:
        copy.wait()
    total[...] = total[...] + extra[...]
    store = pltpu.make_async_copy(total, ancestor, total_sems.at[0])
    store.start()
    pair.run(order, groups(outs, 2), total)
    store.wait()


def first_pairs(place, order, left, own, theirs):
    n = left[0].shape[0]
    block = pltpu.VMEM((2, n, n), F32)
    pair = pltpu.SemaphoreType.DMA((2,))

    def body(place, *refs):
        ins, outs = refs[: len(left) + 2], refs[len(left) + 2 :]
        first_kernel(order, place, *ins, *outs)

    return pl.pallas_call(
        body,
        out_shape=(shaped(2, n, n),) + (shaped(n // 2, n),) * (4 * len(order)),
        in_specs=[SMEM] + [HBM] * (len(left) + 2),
        out_specs=(HBM,) + (VMEM,) * (4 * len(order)),
        scratch_shapes=[block, block, block, pair, pair],
        compiler_params=PARAMS,
        cost_estimate=cost(2, n),
    )(place, *left, own, theirs)


def pair_kernel(order, place, *refs):
    left, (right,), outs, (buffer, total, sems, sem) = unpack(refs, (2 * NY, 1, 4 * len(order)))
    pair = Pair(Place(place), left, buffer, sems)
    pair.start(2 * order[0])
    pair.start(2 * order[0] + 1)
    load(right, total, sem)
    pair.run(order, groups(outs, 2), total)


def pairs(place, order, left, right, dots):
    n = left[0].shape[0]
    block = pltpu.VMEM((2, n, n), F32)
    outs = pl.pallas_call(
        functools.partial(pair_kernel, order),
        out_shape=(shaped(n // 2, n),) * (4 * len(order)),
        in_specs=[SMEM] + [HBM] * (len(left) + 1),
        out_specs=(VMEM,) * (4 * len(order)),
        scratch_shapes=[block, block, pltpu.SemaphoreType.DMA((2,)), pltpu.SemaphoreType.DMA],
        compiler_params=PARAMS,
        cost_estimate=cost(dots, n),
    )(place, *left, right)
    return groups(outs, 4)


def cross_kernel(place, mask, total, out, buffer, sem):
    here = Place(place)
    copy = pltpu.make_async_copy(total.at[here.zh], buffer, sem)
    copy.start()
    copy.wait()
    h = buffer.shape[0] // 2
    for i in range(2):
        for j in range(2):
            rows, cols = slice(i * h, (i + 1) * h), slice(j * h, (j + 1) * h)
            out[0, rows, cols] = -(buffer[rows, cols] * mask[0, i, j].astype(F32))


def cross_block(place, mask, total):
    n = total.shape[1]
    return pl.pallas_call(
        cross_kernel,
        out_shape=shaped(1, n, n),
        in_specs=[SMEM, SMEM, HBM],
        out_specs=VMEM,
        scratch_shapes=[pltpu.VMEM((n, n), F32), pltpu.SemaphoreType.DMA],
        compiler_params=SMALL,
        cost_estimate=light(n),
    )(place, mask, total)


def from_all_y(part):
    return [part] + [lax.ppermute(part, "y", [(y, (y + k) % NY) for y in range(NY)]) for k in range(1, NY)]


def per_device(root_inverse, lower_panel, panel_mask, factor_inverse):
    place = jnp.stack([lax.axis_index(name) for name in AXES]).astype(jnp.int32)
    core, zh = lax.axis_index("core"), lax.axis_index("z_hi")
    away = swap(root_inverse, "z_hi")
    mine, turned, away = lax.optimization_barrier((*masked_block(panel_mask, lower_panel), away))

    good = core == zh
    kept, sent = jnp.where(good, root_inverse, away), jnp.where(good, away, root_inverse)
    pieces = from_all_y(jnp.stack([kept, swap(sent, "core")]))
    groups_of = [[jnp.stack(pieces[:2])], [jnp.stack(pieces[2:])]]

    ring, rows_near, rows_far = [mine], [turned], []
    had, totals = (0, 0), ()
    for r in range(1, NZ + 1):
        ends = []
        if r < NZ:
            ring.append(z_step(ring[-1]))
            ends.append(ring)
        if r == 2:
            ends += groups_of
        if r > 2:
            group = groups_of[(r - 3) % 2]
            group.append(x_step(group[-1]))
            rows = rows_near if r < 6 else rows_far
            rows.append(y_step(rows[-1]))
            ends += [group, rows]
        values = [into[-1] for into in ends]
        if r in HAVE:
            roots = list(zip(*groups_of))
            totals = accumulate(place, HAVE[r], had, roots, ring, totals)
            had = HAVE[r]
            totals, values = lax.optimization_barrier((totals, values))
        else:
            values = lax.optimization_barrier(values)
        for into, value in zip(ends, values):
            into[-1] = value
        if r == NL:
            rows_far = [turned_block(ring[NL])]
    roots = list(zip(*groups_of))
    own, theirs = accumulate(place, (NX, NZ), had, roots, ring, totals)

    rows = rows_near + rows_far
    total, *outs = first_pairs(place, [NL - 1, NL - 2], rows, own, swap(theirs, "core"))
    cross = cross_block(place, panel_mask, total)
    out, *outs = groups(outs, 4)
    moving = [own + theirs for own, theirs in zip(out[2:], swap_both(out[:2]))]
    moving, total = lax.optimization_barrier((moving, total))
    moving = [z_step(half) for half in moving]
    outs += pairs(place, list(range(NL - 3, -1, -1)), rows, total, 0)
    for out in outs[:-1]:
        moving = [z_step(a + own + theirs) for a, own, theirs in zip(moving, out[2:], swap_both(out[:2]))]
    out = outs[-1]
    rest = [a + own + theirs for a, own, theirs in zip(moving, out[2:], swap_both(out[:2]))]
    return cross, factor_inverse + jnp.concatenate(rest, 0)[None]


def solution(mesh):
    split_mesh = Mesh(mesh.devices.reshape(NX, NL, 2, NH, NY), AXES)
    row = ("z_lo", "core")
    block = P("leaf", row, COL)
    return jax.shard_map(
        per_device,
        mesh=split_mesh,
        in_specs=(P(row, ("leaf",) + COL), block, block, block),
        out_specs=(block, block),
        check_vma=False,
    )
```

```python
import functools

import jax
import jax.numpy as jnp
from jax import lax
from jax.experimental import pallas as pl
from jax.experimental.pallas import tpu as pltpu
from jax.sharding import Mesh
from jax.sharding import PartitionSpec as P

AXES = ("leaf", "z_lo", "core", "z_hi", "y")
COL = ("z_hi", "y")
NX, NL, NH, NY = 4, 4, 2, 4
NZ = NL * NH
F32 = jnp.float32
HBM = pl.BlockSpec(memory_space=pltpu.HBM)
SMEM = pl.BlockSpec(memory_space=pltpu.SMEM)
VMEM = pl.BlockSpec(memory_space=pltpu.VMEM)
PARAMS = pltpu.CompilerParams(vmem_limit_bytes=56 << 20)
SMALL = pltpu.CompilerParams(vmem_limit_bytes=16 << 20)


def way(core):
    return 1 if core == 0 else -1


def z_step(block):
    def place(z, core):
        return ((z % NL) * 2 + core) * NH + z // NL

    pairs = [(place(z, core), place((z + way(core)) % NZ, core)) for z in range(NZ) for core in range(2)]
    return lax.ppermute(block, ("z_lo", "core", "z_hi"), pairs)


def y_step(block):
    pairs = [(core * NY + y, core * NY + (y + way(core)) % NY) for y in range(NY) for core in range(2)]
    return lax.ppermute(block, ("core", "y"), pairs)


def x_step(block):
    pairs = [(x * 2 + core, (x + way(core)) % NX * 2 + core) for x in range(NX) for core in range(2)]
    return lax.ppermute(block, ("leaf", "core"), pairs)


def swap(block, axis):
    return lax.ppermute(block, axis, [(0, 1), (1, 0)])


def swap_both(halves):
    return [swap(half, "core") for half in halves]


def split(value):
    high = value.astype(jnp.bfloat16)
    return high, (value - high.astype(F32)).astype(jnp.bfloat16)


def products(lefts, right):
    dot = functools.partial(jnp.dot, preferred_element_type=F32)
    right_high, right_low = split(right)
    outs = []
    for left in lefts:
        left_high, left_low = split(left)
        outs.append(dot(left_high, right_high) + (dot(left_high, right_low) + dot(left_low, right_high)))
    return outs


def cost(dots, n):
    return pl.CostEstimate(flops=6 * dots * n**3, bytes_accessed=12 * dots * n * n, transcendentals=0)


def light(n):
    return pl.CostEstimate(flops=n * n, bytes_accessed=12 * n * n, transcendentals=0)


def shaped(*shape):
    return jax.ShapeDtypeStruct(shape, F32)


class Place:
    def __init__(self, ref):
        self.x, self.zl, self.core, self.zh, self.y = (ref[i] for i in range(5))
        self.z = self.zh * NL + self.zl
        self.turn = 1 - 2 * self.core


def mask_kernel(mask, panel, out, turned):
    h = out.shape[0] // 2
    for i in range(2):
        for j in range(2):
            rows, cols = slice(i * h, (i + 1) * h), slice(j * h, (j + 1) * h)
            part = panel[0, rows, cols] * mask[0, i, j].astype(F32)
            out[rows, cols] = part
            turned[cols, rows] = part.T


def masked_block(mask, panel):
    n = panel.shape[1]
    return pl.pallas_call(
        mask_kernel,
        out_shape=(shaped(n, n), shaped(n, n)),
        in_specs=[SMEM, VMEM],
        out_specs=(VMEM, VMEM),
        compiler_params=SMALL,
        cost_estimate=light(n),
    )(mask, panel)


def turn_kernel(block, turned):
    turned[...] = block[...].T


def turned_block(block):
    n = block.shape[0]
    return pl.pallas_call(
        turn_kernel,
        out_shape=shaped(n, n),
        in_specs=[VMEM],
        out_specs=VMEM,
        compiler_params=SMALL,
        cost_estimate=light(n),
    )(block)


class Step:
    def __init__(self, here, have, had, c):
        self.arrival = have[0] - 1 - c // 2
        from_x = here.x - here.turn * self.arrival
        self.s = jnp.bitwise_and(here.turn * (here.z - from_x), NL - 1) + NL * lax.rem(c, 2)
        self.half = jnp.bitwise_and(here.z - here.turn * self.s, NZ - 1) // NL
        before = jnp.logical_and(self.arrival < had[0], self.s < had[1])
        self.ready = jnp.logical_and(self.s < have[1], jnp.logical_not(before))


class Gather:
    def __init__(self, here, have, had, roots, ring, buffers):
        self.here, self.have, self.had, self.roots, self.ring = here, have, had, roots, ring
        self.left_buffer, self.right_buffer, self.left_sems, self.right_sems = buffers

    def step(self, c):
        return Step(self.here, self.have, self.had, c)

    def start(self, c, slot):
        here, step = self.here, self.step(c)
        left, right = self.left_buffer, self.right_buffer

        @pl.when(step.ready)
        def _():
            for t, pieces in enumerate(self.roots):

                @pl.when(step.arrival == t)
                def _():
                    q = pieces[0].shape[3]
                    for p in range(NY):
                        at = pl.multiple_of(jnp.bitwise_and(here.y - p, NY - 1) * q, q)
                        source, to = pieces[p // 2].at[p % 2], left.at[slot, :, :, pl.ds(at, q)]
                        pltpu.make_async_copy(source, to, self.left_sems.at[slot]).start()

            for k, block in enumerate(self.ring):

                @pl.when(step.s == k)
                def _():
                    pltpu.make_async_copy(block, right.at[slot], self.right_sems.at[slot]).start()

    def run(self, totals):
        steps = 2 * self.have[0]

        @pl.loop(0, steps)
        def _(c):
            slot = lax.rem(c, 2)

            @pl.when(c + 1 < steps)
            def _():
                self.start(c + 1, 1 - slot)

            step = self.step(c)

            @pl.when(step.ready)
            def _():
                for buffer, sems in ((self.left_buffer, self.left_sems), (self.right_buffer, self.right_sems)):
                    pltpu.make_async_copy(buffer.at[slot], buffer.at[slot], sems.at[slot]).wait()
                left = self.left_buffer
                for total, out in zip(totals, products((left[slot, 0], left[slot, 1]), self.right_buffer[slot])):
                    total[step.half] = total[step.half] + out


class Pair:
    def __init__(self, here, left, buffer, sems):
        self.here, self.left, self.buffer, self.sems = here, left, buffer, sems

    def target(self, i):
        here = self.here
        own = lax.rem(i, 2)
        to_z = jnp.bitwise_and(here.z + here.turn * (2 * own - 1) * (i // 2), NZ - 1)
        return jnp.bitwise_and(to_z, NL - 1) * 2 + jnp.where(own == 1, here.core, 1 - here.core), to_z // NL

    def start(self, i):
        here = self.here
        block, _ = self.target(i)
        step = jnp.bitwise_and(here.turn * (here.y - jnp.bitwise_and(block, NY - 1)), NY - 1)
        index = jnp.where(block // NY == here.zh, step, step + NY)
        slot = lax.rem(i, 2)
        for k, ref in enumerate(self.left):

            @pl.when(index == k)
            def _():
                pltpu.make_async_copy(ref, self.buffer.at[slot], self.sems.at[slot]).start()

    def run(self, order, outs, total):
        first, last = 2 * order[0], 2 * order[-1]

        @pl.loop(0, 2 * len(order))
        def _(k):
            i = first - k // 2 * 2 + lax.rem(k, 2)
            slot = lax.rem(k, 2)
            pltpu.make_async_copy(self.buffer.at[slot], self.buffer.at[slot], self.sems.at[slot]).wait()
            (out,) = products((self.buffer[slot],), total[self.target(i)[1]])
            for j, (top, bottom) in enumerate(outs):
                h = top.shape[0]

                @pl.when(k == j)
                def _():
                    top[...] = out[:h]
                    bottom[...] = out[h:]

            @pl.when(i - 2 >= last)
            def _():
                self.start(i - 2)


def unpack(refs, sizes):
    parts = []
    for size in sizes:
        parts.append(refs[:size])
        refs = refs[size:]
    return parts + [refs]


def groups(refs, size):
    return [refs[i : i + size] for i in range(0, len(refs), size)]


def load(source, target, sem):
    copy = pltpu.make_async_copy(source, target, sem)
    copy.start()
    copy.wait()


def gather_kernel(have, had, place, *refs):
    roots, ring, before, afters, rest = unpack(refs, (2 * have[0], have[1], 2 if had[1] else 0, 2))
    left_buffer, right_buffer, own, theirs, left_sems, right_sems, sems = rest
    totals = (own, theirs)
    buffers = (left_buffer, right_buffer, left_sems, right_sems)
    gather = Gather(Place(place), have, had, groups(roots, 2), ring, buffers)
    gather.start(0, 0)
    loads = [pltpu.make_async_copy(ref, total, sems.at[k]) for k, (ref, total) in enumerate(zip(before, totals))]
    for copy in loads:
        copy.start()
    for copy in loads:
        copy.wait()
    if not loads:
        for total in totals:
            total[...] = jnp.zeros_like(total)
    gather.run(totals)
    stores = [pltpu.make_async_copy(total, ref, sems.at[k]) for k, (ref, total) in enumerate(zip(afters, totals))]
    for copy in stores:
        copy.start()
    for copy in stores:
        copy.wait()


def accumulate(place, have, had, roots, ring, totals):
    n = ring[0].shape[0]
    operands = [place] + [part for pieces in roots[: have[0]] for part in pieces]
    operands += ring[: have[1]]
    aliases = {}
    if had[1]:
        aliases = {len(operands): 0, len(operands) + 1: 1}
        operands += totals
    block = pltpu.VMEM((2, n, n), F32)
    pair = pltpu.SemaphoreType.DMA((2,))
    return pl.pallas_call(
        functools.partial(gather_kernel, have, had),
        out_shape=(shaped(2, n, n),) * 2,
        in_specs=[SMEM] + [HBM] * (len(operands) - 1),
        out_specs=(HBM,) * 2,
        scratch_shapes=[pltpu.VMEM((2, 2, n, n), F32), block, block, block, pair, pair, pair],
        input_output_aliases=aliases,
        compiler_params=PARAMS,
        cost_estimate=cost(6, n),
    )(*operands)


def first_kernel(order, place, *refs):
    left, (own, theirs, ancestor), outs, (buffer, total, extra, sems, total_sems) = unpack(refs, (2 * NY, 3, 4 * len(order)))
    pair = Pair(Place(place), left, buffer, sems)
    pair.start(2 * order[0])
    pair.start(2 * order[0] + 1)
    loads = [pltpu.make_async_copy(a, b, total_sems.at[k]) for k, (a, b) in enumerate(((own, total), (theirs, extra)))]
    for copy in loads:
        copy.start()
    for copy in loads:
        copy.wait()
    total[...] = total[...] + extra[...]
    store = pltpu.make_async_copy(total, ancestor, total_sems.at[0])
    store.start()
    pair.run(order, groups(outs, 2), total)
    store.wait()


def first_pairs(place, order, left, own, theirs):
    n = left[0].shape[0]
    block = pltpu.VMEM((2, n, n), F32)
    pair = pltpu.SemaphoreType.DMA((2,))

    def body(place, *refs):
        ins, outs = refs[: len(left) + 2], refs[len(left) + 2 :]
        first_kernel(order, place, *ins, *outs)

    return pl.pallas_call(
        body,
        out_shape=(shaped(2, n, n),) + (shaped(n // 2, n),) * (4 * len(order)),
        in_specs=[SMEM] + [HBM] * (len(left) + 2),
        out_specs=(HBM,) + (VMEM,) * (4 * len(order)),
        scratch_shapes=[block, block, block, pair, pair],
        compiler_params=PARAMS,
        cost_estimate=cost(2, n),
    )(place, *left, own, theirs)


def pair_kernel(order, place, *refs):
    left, (right,), outs, (buffer, total, sems, sem) = unpack(refs, (2 * NY, 1, 4 * len(order)))
    pair = Pair(Place(place), left, buffer, sems)
    pair.start(2 * order[0])
    pair.start(2 * order[0] + 1)
    load(right, total, sem)
    pair.run(order, groups(outs, 2), total)


def pairs(place, order, left, right, dots):
    n = left[0].shape[0]
    block = pltpu.VMEM((2, n, n), F32)
    outs = pl.pallas_call(
        functools.partial(pair_kernel, order),
        out_shape=(shaped(n // 2, n),) * (4 * len(order)),
        in_specs=[SMEM] + [HBM] * (len(left) + 1),
        out_specs=(VMEM,) * (4 * len(order)),
        scratch_shapes=[block, block, pltpu.SemaphoreType.DMA((2,)), pltpu.SemaphoreType.DMA],
        compiler_params=PARAMS,
        cost_estimate=cost(dots, n),
    )(place, *left, right)
    return groups(outs, 4)


def cross_kernel(place, mask, total, out, buffer, sem):
    here = Place(place)
    copy = pltpu.make_async_copy(total.at[here.zh], buffer, sem)
    copy.start()
    copy.wait()
    h = buffer.shape[0] // 2
    for i in range(2):
        for j in range(2):
            rows, cols = slice(i * h, (i + 1) * h), slice(j * h, (j + 1) * h)
            out[0, rows, cols] = -(buffer[rows, cols] * mask[0, i, j].astype(F32))


def cross_block(place, mask, total):
    n = total.shape[1]
    return pl.pallas_call(
        cross_kernel,
        out_shape=shaped(1, n, n),
        in_specs=[SMEM, SMEM, HBM],
        out_specs=VMEM,
        scratch_shapes=[pltpu.VMEM((n, n), F32), pltpu.SemaphoreType.DMA],
        compiler_params=SMALL,
        cost_estimate=light(n),
    )(place, mask, total)


def from_all_y(part):
    return [part] + [lax.ppermute(part, "y", [(y, (y + k) % NY) for y in range(NY)]) for k in range(1, NY)]


def per_device(root_inverse, lower_panel, panel_mask, factor_inverse):
    place = jnp.stack([lax.axis_index(name) for name in AXES]).astype(jnp.int32)
    core, zh = lax.axis_index("core"), lax.axis_index("z_hi")
    away = swap(root_inverse, "z_hi")
    mine, turned = masked_block(panel_mask, lower_panel)

    good = core == zh
    kept, sent = jnp.where(good, root_inverse, away), jnp.where(good, away, root_inverse)
    piece, mine, turned = lax.optimization_barrier((jnp.stack([kept, swap(sent, "core")]), mine, turned))

    ring, rows_near, rows_far = [mine], [turned], []
    had, totals = (0, 0), ()
    for r in range(NX):
        ends = [ring]
        ring.append(z_step(ring[-1]))
        if r == 0:
            pieces = from_all_y(piece)
            ring[1], pieces[1], pieces[3] = lax.optimization_barrier((ring[1], pieces[1], pieces[3]))
        if len(ring) < NZ:
            ring.append(z_step(ring[-1]))
        if r == 0:
            groups_of = [[jnp.stack(pieces[:2])], [jnp.stack(pieces[2:])]]
        else:
            for group in groups_of:
                group.append(x_step(group[-1]))
            for _ in range(2):
                rows = rows_near if len(rows_near) < NY else rows_far
                rows.append(y_step(rows[-1]))
            ends += [rows_near] if r == 1 else [rows_near, rows_far] if r == 2 else [rows_far]
        ends += groups_of
        values = [into[-1] for into in ends]
        if r == NX - 1:
            had = (NX - 1, NZ - 1)
            totals = accumulate(place, had, (0, 0), list(zip(*groups_of)), ring, totals)
            totals, values = lax.optimization_barrier((totals, values))
        else:
            values = lax.optimization_barrier(values)
        for into, value in zip(ends, values):
            into[-1] = value
        if r == 1:
            rows_far = [turned_block(ring[NL])]
    roots = list(zip(*groups_of))
    own, theirs = accumulate(place, (NX, NZ), had, roots, ring, totals)

    rows = rows_near + rows_far
    total, *outs = first_pairs(place, [NL - 1, NL - 2], rows, own, swap(theirs, "core"))
    cross = cross_block(place, panel_mask, total)
    out, *outs = groups(outs, 4)
    moving = [own + theirs for own, theirs in zip(out[2:], swap_both(out[:2]))]
    moving, total = lax.optimization_barrier((moving, total))
    moving = [z_step(half) for half in moving]
    outs += pairs(place, list(range(NL - 3, -1, -1)), rows, total, 0)
    for out in outs[:-1]:
        moving = [z_step(a + own + theirs) for a, own, theirs in zip(moving, out[2:], swap_both(out[:2]))]
    out = outs[-1]
    rest = [a + own + theirs for a, own, theirs in zip(moving, out[2:], swap_both(out[:2]))]
    return cross, factor_inverse + jnp.concatenate(rest, 0)[None]


def solution(mesh):
    split_mesh = Mesh(mesh.devices.reshape(NX, NL, 2, NH, NY), AXES)
    row = ("z_lo", "core")
    block = P("leaf", row, COL)
    return jax.shard_map(
        per_device,
        mesh=split_mesh,
        in_specs=(P(row, ("leaf",) + COL), block, block, block),
        out_specs=(block, block),
        check_vma=False,
    )
```

```python
import functools

import jax
import jax.numpy as jnp
from jax import lax
from jax.experimental import pallas as pl
from jax.experimental.pallas import tpu as pltpu
from jax.sharding import Mesh
from jax.sharding import PartitionSpec as P

AXES = ("leaf", "z_lo", "core", "z_hi", "y")
COL = ("z_hi", "y")
NX, NL, NH, NY = 4, 4, 2, 4
NZ = NL * NH
F32 = jnp.float32
HBM = pl.BlockSpec(memory_space=pltpu.HBM)
SMEM = pl.BlockSpec(memory_space=pltpu.SMEM)
VMEM = pl.BlockSpec(memory_space=pltpu.VMEM)
PARAMS = pltpu.CompilerParams(vmem_limit_bytes=56 << 20)
SMALL = pltpu.CompilerParams(vmem_limit_bytes=16 << 20)


def way(core):
    return 1 if core == 0 else -1


def z_step(block):
    def place(z, core):
        return ((z % NL) * 2 + core) * NH + z // NL

    pairs = [(place(z, core), place((z + way(core)) % NZ, core)) for z in range(NZ) for core in range(2)]
    return lax.ppermute(block, ("z_lo", "core", "z_hi"), pairs)


def y_step(block):
    pairs = [(core * NY + y, core * NY + (y + way(core)) % NY) for y in range(NY) for core in range(2)]
    return lax.ppermute(block, ("core", "y"), pairs)


def x_step(block):
    pairs = [(x * 2 + core, (x + way(core)) % NX * 2 + core) for x in range(NX) for core in range(2)]
    return lax.ppermute(block, ("leaf", "core"), pairs)


def swap(block, axis):
    return lax.ppermute(block, axis, [(0, 1), (1, 0)])


def swap_both(halves):
    return [swap(half, "core") for half in halves]


def split(value):
    high = value.astype(jnp.bfloat16)
    return high, (value - high.astype(F32)).astype(jnp.bfloat16)


def products(lefts, right):
    dot = functools.partial(jnp.dot, preferred_element_type=F32)
    right_high, right_low = split(right)
    outs = []
    for left in lefts:
        left_high, left_low = split(left)
        outs.append(dot(left_high, right_high) + (dot(left_high, right_low) + dot(left_low, right_high)))
    return outs


def cost(dots, n):
    return pl.CostEstimate(flops=6 * dots * n**3, bytes_accessed=12 * dots * n * n, transcendentals=0)


def light(n):
    return pl.CostEstimate(flops=n * n, bytes_accessed=12 * n * n, transcendentals=0)


def shaped(*shape):
    return jax.ShapeDtypeStruct(shape, F32)


class Place:
    def __init__(self, ref):
        self.x, self.zl, self.core, self.zh, self.y = (ref[i] for i in range(5))
        self.z = self.zh * NL + self.zl
        self.turn = 1 - 2 * self.core


def mask_kernel(mask, panel, out, turned):
    h = out.shape[0] // 2
    for i in range(2):
        for j in range(2):
            rows, cols = slice(i * h, (i + 1) * h), slice(j * h, (j + 1) * h)
            part = panel[0, rows, cols] * mask[0, i, j].astype(F32)
            out[rows, cols] = part
            turned[cols, rows] = part.T


def masked_block(mask, panel):
    n = panel.shape[1]
    return pl.pallas_call(
        mask_kernel,
        out_shape=(shaped(n, n), shaped(n, n)),
        in_specs=[SMEM, VMEM],
        out_specs=(VMEM, VMEM),
        compiler_params=SMALL,
        cost_estimate=light(n),
    )(mask, panel)


def turn_kernel(block, turned):
    turned[...] = block[...].T


def turned_block(block):
    n = block.shape[0]
    return pl.pallas_call(
        turn_kernel,
        out_shape=shaped(n, n),
        in_specs=[VMEM],
        out_specs=VMEM,
        compiler_params=SMALL,
        cost_estimate=light(n),
    )(block)


class Step:
    def __init__(self, here, have, had, c):
        self.arrival = have[0] - 1 - c // 2
        from_x = here.x - here.turn * self.arrival
        self.s = jnp.bitwise_and(here.turn * (here.z - from_x), NL - 1) + NL * lax.rem(c, 2)
        self.half = jnp.bitwise_and(here.z - here.turn * self.s, NZ - 1) // NL
        before = jnp.logical_and(self.arrival < had[0], self.s < had[1])
        self.ready = jnp.logical_and(self.s < have[1], jnp.logical_not(before))


class Gather:
    def __init__(self, here, have, had, roots, ring, buffers):
        self.here, self.have, self.had, self.roots, self.ring = here, have, had, roots, ring
        self.left_buffer, self.right_buffer, self.left_sems, self.right_sems = buffers

    def step(self, c):
        return Step(self.here, self.have, self.had, c)

    def start(self, c, slot):
        here, step = self.here, self.step(c)
        left, right = self.left_buffer, self.right_buffer

        @pl.when(step.ready)
        def _():
            for t, pieces in enumerate(self.roots):

                @pl.when(step.arrival == t)
                def _():
                    q = pieces[0].shape[3]
                    for p in range(NY):
                        at = pl.multiple_of(jnp.bitwise_and(here.y - p, NY - 1) * q, q)
                        source, to = pieces[p // 2].at[p % 2], left.at[slot, :, :, pl.ds(at, q)]
                        pltpu.make_async_copy(source, to, self.left_sems.at[slot]).start()

            for k, block in enumerate(self.ring):

                @pl.when(step.s == k)
                def _():
                    pltpu.make_async_copy(block, right.at[slot], self.right_sems.at[slot]).start()

    def run(self, totals):
        steps = 2 * self.have[0]

        @pl.loop(0, steps)
        def _(c):
            slot = lax.rem(c, 2)

            @pl.when(c + 1 < steps)
            def _():
                self.start(c + 1, 1 - slot)

            step = self.step(c)

            @pl.when(step.ready)
            def _():
                for buffer, sems in ((self.left_buffer, self.left_sems), (self.right_buffer, self.right_sems)):
                    pltpu.make_async_copy(buffer.at[slot], buffer.at[slot], sems.at[slot]).wait()
                left = self.left_buffer
                for total, out in zip(totals, products((left[slot, 0], left[slot, 1]), self.right_buffer[slot])):
                    total[step.half] = total[step.half] + out


class Pair:
    def __init__(self, here, left, buffer, sems):
        self.here, self.left, self.buffer, self.sems = here, left, buffer, sems

    def target(self, i):
        here = self.here
        own = lax.rem(i, 2)
        to_z = jnp.bitwise_and(here.z + here.turn * (2 * own - 1) * (i // 2), NZ - 1)
        return jnp.bitwise_and(to_z, NL - 1) * 2 + jnp.where(own == 1, here.core, 1 - here.core), to_z // NL

    def start(self, i):
        here = self.here
        block, _ = self.target(i)
        step = jnp.bitwise_and(here.turn * (here.y - jnp.bitwise_and(block, NY - 1)), NY - 1)
        index = jnp.where(block // NY == here.zh, step, step + NY)
        slot = lax.rem(i, 2)
        for k, ref in enumerate(self.left):

            @pl.when(index == k)
            def _():
                pltpu.make_async_copy(ref, self.buffer.at[slot], self.sems.at[slot]).start()

    def run(self, order, outs, total):
        first, last = 2 * order[0], 2 * order[-1]

        @pl.loop(0, 2 * len(order))
        def _(k):
            i = first - k // 2 * 2 + lax.rem(k, 2)
            slot = lax.rem(k, 2)
            pltpu.make_async_copy(self.buffer.at[slot], self.buffer.at[slot], self.sems.at[slot]).wait()
            (out,) = products((self.buffer[slot],), total[self.target(i)[1]])
            for j, (top, bottom) in enumerate(outs):
                h = top.shape[0]

                @pl.when(k == j)
                def _():
                    top[...] = out[:h]
                    bottom[...] = out[h:]

            @pl.when(i - 2 >= last)
            def _():
                self.start(i - 2)


def unpack(refs, sizes):
    parts = []
    for size in sizes:
        parts.append(refs[:size])
        refs = refs[size:]
    return parts + [refs]


def groups(refs, size):
    return [refs[i : i + size] for i in range(0, len(refs), size)]


def load(source, target, sem):
    copy = pltpu.make_async_copy(source, target, sem)
    copy.start()
    copy.wait()


def gather_kernel(have, had, place, *refs):
    roots, ring, before, afters, rest = unpack(refs, (2 * have[0], have[1], 2 if had[1] else 0, 2))
    left_buffer, right_buffer, own, theirs, left_sems, right_sems, sems = rest
    totals = (own, theirs)
    buffers = (left_buffer, right_buffer, left_sems, right_sems)
    gather = Gather(Place(place), have, had, groups(roots, 2), ring, buffers)
    gather.start(0, 0)
    loads = [pltpu.make_async_copy(ref, total, sems.at[k]) for k, (ref, total) in enumerate(zip(before, totals))]
    for copy in loads:
        copy.start()
    for copy in loads:
        copy.wait()
    if not loads:
        for total in totals:
            total[...] = jnp.zeros_like(total)
    gather.run(totals)
    stores = [pltpu.make_async_copy(total, ref, sems.at[k]) for k, (ref, total) in enumerate(zip(afters, totals))]
    for copy in stores:
        copy.start()
    for copy in stores:
        copy.wait()


def accumulate(place, have, had, roots, ring, totals):
    n = ring[0].shape[0]
    operands = [place] + [part for pieces in roots[: have[0]] for part in pieces]
    operands += ring[: have[1]]
    aliases = {}
    if had[1]:
        aliases = {len(operands): 0, len(operands) + 1: 1}
        operands += totals
    block = pltpu.VMEM((2, n, n), F32)
    pair = pltpu.SemaphoreType.DMA((2,))
    return pl.pallas_call(
        functools.partial(gather_kernel, have, had),
        out_shape=(shaped(2, n, n),) * 2,
        in_specs=[SMEM] + [HBM] * (len(operands) - 1),
        out_specs=(HBM,) * 2,
        scratch_shapes=[pltpu.VMEM((2, 2, n, n), F32), block, block, block, pair, pair, pair],
        input_output_aliases=aliases,
        compiler_params=PARAMS,
        cost_estimate=cost(6, n),
    )(*operands)


def first_kernel(order, place, *refs):
    left, (own, theirs, ancestor), outs, (buffer, total, extra, sems, total_sems) = unpack(refs, (2 * NY, 3, 4 * len(order)))
    pair = Pair(Place(place), left, buffer, sems)
    pair.start(2 * order[0])
    pair.start(2 * order[0] + 1)
    loads = [pltpu.make_async_copy(a, b, total_sems.at[k]) for k, (a, b) in enumerate(((own, total), (theirs, extra)))]
    for copy in loads:
        copy.start()
    for copy in loads:
        copy.wait()
    total[...] = total[...] + extra[...]
    store = pltpu.make_async_copy(total, ancestor, total_sems.at[0])
    store.start()
    pair.run(order, groups(outs, 2), total)
    store.wait()


def first_pairs(place, order, left, own, theirs):
    n = left[0].shape[0]
    block = pltpu.VMEM((2, n, n), F32)
    pair = pltpu.SemaphoreType.DMA((2,))

    def body(place, *refs):
        ins, outs = refs[: len(left) + 2], refs[len(left) + 2 :]
        first_kernel(order, place, *ins, *outs)

    return pl.pallas_call(
        body,
        out_shape=(shaped(2, n, n),) + (shaped(n // 2, n),) * (4 * len(order)),
        in_specs=[SMEM] + [HBM] * (len(left) + 2),
        out_specs=(HBM,) + (VMEM,) * (4 * len(order)),
        scratch_shapes=[block, block, block, pair, pair],
        compiler_params=PARAMS,
        cost_estimate=cost(2, n),
    )(place, *left, own, theirs)


def pair_kernel(order, place, *refs):
    left, (right,), outs, (buffer, total, sems, sem) = unpack(refs, (2 * NY, 1, 4 * len(order)))
    pair = Pair(Place(place), left, buffer, sems)
    pair.start(2 * order[0])
    pair.start(2 * order[0] + 1)
    load(right, total, sem)
    pair.run(order, groups(outs, 2), total)


def pairs(place, order, left, right, dots):
    n = left[0].shape[0]
    block = pltpu.VMEM((2, n, n), F32)
    outs = pl.pallas_call(
        functools.partial(pair_kernel, order),
        out_shape=(shaped(n // 2, n),) * (4 * len(order)),
        in_specs=[SMEM] + [HBM] * (len(left) + 1),
        out_specs=(VMEM,) * (4 * len(order)),
        scratch_shapes=[block, block, pltpu.SemaphoreType.DMA((2,)), pltpu.SemaphoreType.DMA],
        compiler_params=PARAMS,
        cost_estimate=cost(dots, n),
    )(place, *left, right)
    return groups(outs, 4)


def cross_kernel(place, mask, total, out, buffer, sem):
    here = Place(place)
    copy = pltpu.make_async_copy(total.at[here.zh], buffer, sem)
    copy.start()
    copy.wait()
    h = buffer.shape[0] // 2
    for i in range(2):
        for j in range(2):
            rows, cols = slice(i * h, (i + 1) * h), slice(j * h, (j + 1) * h)
            out[0, rows, cols] = -(buffer[rows, cols] * mask[0, i, j].astype(F32))


def cross_block(place, mask, total):
    n = total.shape[1]
    return pl.pallas_call(
        cross_kernel,
        out_shape=shaped(1, n, n),
        in_specs=[SMEM, SMEM, HBM],
        out_specs=VMEM,
        scratch_shapes=[pltpu.VMEM((n, n), F32), pltpu.SemaphoreType.DMA],
        compiler_params=SMALL,
        cost_estimate=light(n),
    )(place, mask, total)


def from_all_y(part):
    return [part] + [lax.ppermute(part, "y", [(y, (y + k) % NY) for y in range(NY)]) for k in range(1, NY)]


def per_device(root_inverse, lower_panel, panel_mask, factor_inverse):
    place = jnp.stack([lax.axis_index(name) for name in AXES]).astype(jnp.int32)
    core, zh = lax.axis_index("core"), lax.axis_index("z_hi")
    away = swap(root_inverse, "z_hi")
    mine, turned = masked_block(panel_mask, lower_panel)

    good = core == zh
    kept, sent = jnp.where(good, root_inverse, away), jnp.where(good, away, root_inverse)
    piece = jnp.stack([kept, swap(sent, "core")])
    piece, mine, moved = lax.optimization_barrier((piece, mine, y_step(turned)))

    ring, rows_near, rows_far = [mine], [turned, moved], []
    had, totals = (0, 0), ()
    for r in range(NX):
        ends = [ring]
        ring.append(z_step(ring[-1]))
        if r == 0:
            pieces = from_all_y(piece)
            ring[1], pieces[1], pieces[3] = lax.optimization_barrier((ring[1], pieces[1], pieces[3]))
        if len(ring) < NZ:
            ring.append(z_step(ring[-1]))
        if r == 0:
            groups_of = [[jnp.stack(pieces[:2])], [jnp.stack(pieces[2:])]]
        else:
            for group in groups_of:
                group.append(x_step(group[-1]))
            rows = rows_near if r == 1 else rows_far
            for _ in range(min(2, NY - len(rows))):
                rows.append(y_step(rows[-1]))
            ends.append(rows)
        ends += groups_of + ([rows_near] if r == 0 else [])
        values = [into[-1] for into in ends]
        if r == NX - 1:
            had = (NX - 1, NZ - 1)
            totals = accumulate(place, had, (0, 0), list(zip(*groups_of)), ring, totals)
            totals, values = lax.optimization_barrier((totals, values))
        else:
            values = lax.optimization_barrier(values)
        for into, value in zip(ends, values):
            into[-1] = value
        if r == 1:
            rows_far = [turned_block(ring[NL])]
    roots = list(zip(*groups_of))
    own, theirs = accumulate(place, (NX, NZ), had, roots, ring, totals)

    rows = rows_near + rows_far
    total, *outs = first_pairs(place, [NL - 1, NL - 2], rows, own, swap(theirs, "core"))
    cross = cross_block(place, panel_mask, total)
    out, *outs = groups(outs, 4)
    moving = [own + theirs for own, theirs in zip(out[2:], swap_both(out[:2]))]
    moving, total = lax.optimization_barrier((moving, total))
    moving = [z_step(half) for half in moving]
    outs += pairs(place, list(range(NL - 3, -1, -1)), rows, total, 0)
    for out in outs[:-1]:
        moving = [z_step(a + own + theirs) for a, own, theirs in zip(moving, out[2:], swap_both(out[:2]))]
    out = outs[-1]
    rest = [a + own + theirs for a, own, theirs in zip(moving, out[2:], swap_both(out[:2]))]
    return cross, factor_inverse + jnp.concatenate(rest, 0)[None]


def solution(mesh):
    split_mesh = Mesh(mesh.devices.reshape(NX, NL, 2, NH, NY), AXES)
    row = ("z_lo", "core")
    block = P("leaf", row, COL)
    return jax.shard_map(
        per_device,
        mesh=split_mesh,
        in_specs=(P(row, ("leaf",) + COL), block, block, block),
        out_specs=(block, block),
        check_vma=False,
    )
```

```python
import functools

import jax
import jax.numpy as jnp
from jax import lax
from jax.experimental import pallas as pl
from jax.experimental.pallas import tpu as pltpu
from jax.sharding import Mesh
from jax.sharding import PartitionSpec as P

AXES = ("leaf", "z_lo", "core", "z_hi", "y")
COL = ("z_hi", "y")
NX, NL, NH, NY = 4, 4, 2, 4
NZ = NL * NH
F32 = jnp.float32
HBM = pl.BlockSpec(memory_space=pltpu.HBM)
SMEM = pl.BlockSpec(memory_space=pltpu.SMEM)
VMEM = pl.BlockSpec(memory_space=pltpu.VMEM)
PARAMS = pltpu.CompilerParams(vmem_limit_bytes=56 << 20)
SMALL = pltpu.CompilerParams(vmem_limit_bytes=16 << 20)


def way(core):
    return 1 if core == 0 else -1


def z_step(block):
    def place(z, core):
        return ((z % NL) * 2 + core) * NH + z // NL

    pairs = [(place(z, core), place((z + way(core)) % NZ, core)) for z in range(NZ) for core in range(2)]
    return lax.ppermute(block, ("z_lo", "core", "z_hi"), pairs)


def y_step(block):
    pairs = [(core * NY + y, core * NY + (y + way(core)) % NY) for y in range(NY) for core in range(2)]
    return lax.ppermute(block, ("core", "y"), pairs)


def x_step(block):
    pairs = [(x * 2 + core, (x + way(core)) % NX * 2 + core) for x in range(NX) for core in range(2)]
    return lax.ppermute(block, ("leaf", "core"), pairs)


def swap(block, axis):
    return lax.ppermute(block, axis, [(0, 1), (1, 0)])


def swap_both(halves):
    return [swap(half, "core") for half in halves]


def split(value):
    high = value.astype(jnp.bfloat16)
    return high, (value - high.astype(F32)).astype(jnp.bfloat16)


def products(lefts, right):
    dot = functools.partial(jnp.dot, preferred_element_type=F32)
    right_high, right_low = split(right)
    outs = []
    for left in lefts:
        left_high, left_low = split(left)
        outs.append(dot(left_high, right_high) + (dot(left_high, right_low) + dot(left_low, right_high)))
    return outs


def cost(dots, n):
    return pl.CostEstimate(flops=6 * dots * n**3, bytes_accessed=12 * dots * n * n, transcendentals=0)


def light(n):
    return pl.CostEstimate(flops=n * n, bytes_accessed=12 * n * n, transcendentals=0)


def shaped(*shape):
    return jax.ShapeDtypeStruct(shape, F32)


class Place:
    def __init__(self, ref):
        self.x, self.zl, self.core, self.zh, self.y = (ref[i] for i in range(5))
        self.z = self.zh * NL + self.zl
        self.turn = 1 - 2 * self.core


def mask_kernel(mask, panel, out, turned):
    h = out.shape[0] // 2
    for i in range(2):
        for j in range(2):
            rows, cols = slice(i * h, (i + 1) * h), slice(j * h, (j + 1) * h)
            part = panel[0, rows, cols] * mask[0, i, j].astype(F32)
            out[rows, cols] = part
            turned[cols, rows] = part.T


def masked_block(mask, panel):
    n = panel.shape[1]
    return pl.pallas_call(
        mask_kernel,
        out_shape=(shaped(n, n), shaped(n, n)),
        in_specs=[SMEM, VMEM],
        out_specs=(VMEM, VMEM),
        compiler_params=SMALL,
        cost_estimate=light(n),
    )(mask, panel)


def turn_kernel(block, turned):
    turned[...] = block[...].T


def turned_block(block):
    n = block.shape[0]
    return pl.pallas_call(
        turn_kernel,
        out_shape=shaped(n, n),
        in_specs=[VMEM],
        out_specs=VMEM,
        compiler_params=SMALL,
        cost_estimate=light(n),
    )(block)


class Step:
    def __init__(self, here, have, had, c):
        self.arrival = have[0] - 1 - c // 2
        from_x = here.x - here.turn * self.arrival
        self.s = jnp.bitwise_and(here.turn * (here.z - from_x), NL - 1) + NL * lax.rem(c, 2)
        self.half = jnp.bitwise_and(here.z - here.turn * self.s, NZ - 1) // NL
        before = jnp.logical_and(self.arrival < had[0], self.s < had[1])
        self.ready = jnp.logical_and(self.s < have[1], jnp.logical_not(before))


class Gather:
    def __init__(self, here, have, had, roots, ring, buffers):
        self.here, self.have, self.had, self.roots, self.ring = here, have, had, roots, ring
        self.left_buffer, self.right_buffer, self.left_sems, self.right_sems = buffers

    def step(self, c):
        return Step(self.here, self.have, self.had, c)

    def start(self, c, slot):
        here, step = self.here, self.step(c)
        left, right = self.left_buffer, self.right_buffer

        @pl.when(step.ready)
        def _():
            for t, pieces in enumerate(self.roots):

                @pl.when(step.arrival == t)
                def _():
                    q = pieces[0].shape[3]
                    for p in range(NY):
                        at = pl.multiple_of(jnp.bitwise_and(here.y - p, NY - 1) * q, q)
                        source, to = pieces[p // 2].at[p % 2], left.at[slot, :, :, pl.ds(at, q)]
                        pltpu.make_async_copy(source, to, self.left_sems.at[slot]).start()

            for k, block in enumerate(self.ring):

                @pl.when(step.s == k)
                def _():
                    pltpu.make_async_copy(block, right.at[slot], self.right_sems.at[slot]).start()

    def run(self, totals):
        steps = 2 * self.have[0]

        @pl.loop(0, steps)
        def _(c):
            slot = lax.rem(c, 2)

            @pl.when(c + 1 < steps)
            def _():
                self.start(c + 1, 1 - slot)

            step = self.step(c)

            @pl.when(step.ready)
            def _():
                for buffer, sems in ((self.left_buffer, self.left_sems), (self.right_buffer, self.right_sems)):
                    pltpu.make_async_copy(buffer.at[slot], buffer.at[slot], sems.at[slot]).wait()
                left = self.left_buffer
                for total, out in zip(totals, products((left[slot, 0], left[slot, 1]), self.right_buffer[slot])):
                    total[step.half] = total[step.half] + out


class Pair:
    def __init__(self, here, left, buffer, sems):
        self.here, self.left, self.buffer, self.sems = here, left, buffer, sems

    def target(self, i):
        here = self.here
        own = lax.rem(i, 2)
        to_z = jnp.bitwise_and(here.z + here.turn * (2 * own - 1) * (i // 2), NZ - 1)
        return jnp.bitwise_and(to_z, NL - 1) * 2 + jnp.where(own == 1, here.core, 1 - here.core), to_z // NL

    def start(self, i):
        here = self.here
        block, _ = self.target(i)
        step = jnp.bitwise_and(here.turn * (here.y - jnp.bitwise_and(block, NY - 1)), NY - 1)
        index = jnp.where(block // NY == here.zh, step, step + NY)
        slot = lax.rem(i, 2)
        for k, ref in enumerate(self.left):

            @pl.when(index == k)
            def _():
                pltpu.make_async_copy(ref, self.buffer.at[slot], self.sems.at[slot]).start()

    def run(self, order, outs, total):
        first, last = 2 * order[0], 2 * order[-1]

        @pl.loop(0, 2 * len(order))
        def _(k):
            i = first - k // 2 * 2 + lax.rem(k, 2)
            slot = lax.rem(k, 2)
            pltpu.make_async_copy(self.buffer.at[slot], self.buffer.at[slot], self.sems.at[slot]).wait()
            (out,) = products((self.buffer[slot],), total[self.target(i)[1]])
            for j, (top, bottom) in enumerate(outs):
                h = top.shape[0]

                @pl.when(k == j)
                def _():
                    top[...] = out[:h]
                    bottom[...] = out[h:]

            @pl.when(i - 2 >= last)
            def _():
                self.start(i - 2)


def unpack(refs, sizes):
    parts = []
    for size in sizes:
        parts.append(refs[:size])
        refs = refs[size:]
    return parts + [refs]


def groups(refs, size):
    return [refs[i : i + size] for i in range(0, len(refs), size)]


def load(source, target, sem):
    copy = pltpu.make_async_copy(source, target, sem)
    copy.start()
    copy.wait()


def gather_kernel(have, had, place, *refs):
    roots, ring, before, afters, rest = unpack(refs, (2 * have[0], have[1], 2 if had[1] else 0, 2))
    left_buffer, right_buffer, own, theirs, left_sems, right_sems, sems = rest
    totals = (own, theirs)
    buffers = (left_buffer, right_buffer, left_sems, right_sems)
    gather = Gather(Place(place), have, had, groups(roots, 2), ring, buffers)
    gather.start(0, 0)
    loads = [pltpu.make_async_copy(ref, total, sems.at[k]) for k, (ref, total) in enumerate(zip(before, totals))]
    for copy in loads:
        copy.start()
    for copy in loads:
        copy.wait()
    if not loads:
        for total in totals:
            total[...] = jnp.zeros_like(total)
    gather.run(totals)
    stores = [pltpu.make_async_copy(total, ref, sems.at[k]) for k, (ref, total) in enumerate(zip(afters, totals))]
    for copy in stores:
        copy.start()
    for copy in stores:
        copy.wait()


def accumulate(place, have, had, roots, ring, totals):
    n = ring[0].shape[0]
    operands = [place] + [part for pieces in roots[: have[0]] for part in pieces]
    operands += ring[: have[1]]
    aliases = {}
    if had[1]:
        aliases = {len(operands): 0, len(operands) + 1: 1}
        operands += totals
    block = pltpu.VMEM((2, n, n), F32)
    pair = pltpu.SemaphoreType.DMA((2,))
    return pl.pallas_call(
        functools.partial(gather_kernel, have, had),
        out_shape=(shaped(2, n, n),) * 2,
        in_specs=[SMEM] + [HBM] * (len(operands) - 1),
        out_specs=(HBM,) * 2,
        scratch_shapes=[pltpu.VMEM((2, 2, n, n), F32), block, block, block, pair, pair, pair],
        input_output_aliases=aliases,
        compiler_params=PARAMS,
        cost_estimate=cost(6, n),
    )(*operands)


def first_kernel(order, place, *refs):
    left, (own, theirs, ancestor), outs, (buffer, total, extra, sems, total_sems) = unpack(refs, (2 * NY, 3, 4 * len(order)))
    pair = Pair(Place(place), left, buffer, sems)
    pair.start(2 * order[0])
    pair.start(2 * order[0] + 1)
    loads = [pltpu.make_async_copy(a, b, total_sems.at[k]) for k, (a, b) in enumerate(((own, total), (theirs, extra)))]
    for copy in loads:
        copy.start()
    for copy in loads:
        copy.wait()
    total[...] = total[...] + extra[...]
    store = pltpu.make_async_copy(total, ancestor, total_sems.at[0])
    store.start()
    pair.run(order, groups(outs, 2), total)
    store.wait()


def first_pairs(place, order, left, own, theirs):
    n = left[0].shape[0]
    block = pltpu.VMEM((2, n, n), F32)
    pair = pltpu.SemaphoreType.DMA((2,))

    def body(place, *refs):
        ins, outs = refs[: len(left) + 2], refs[len(left) + 2 :]
        first_kernel(order, place, *ins, *outs)

    return pl.pallas_call(
        body,
        out_shape=(shaped(2, n, n),) + (shaped(n // 2, n),) * (4 * len(order)),
        in_specs=[SMEM] + [HBM] * (len(left) + 2),
        out_specs=(HBM,) + (VMEM,) * (4 * len(order)),
        scratch_shapes=[block, block, block, pair, pair],
        compiler_params=PARAMS,
        cost_estimate=cost(2, n),
    )(place, *left, own, theirs)


def pair_kernel(order, place, *refs):
    left, (right,), outs, (buffer, total, sems, sem) = unpack(refs, (2 * NY, 1, 4 * len(order)))
    pair = Pair(Place(place), left, buffer, sems)
    pair.start(2 * order[0])
    pair.start(2 * order[0] + 1)
    load(right, total, sem)
    pair.run(order, groups(outs, 2), total)


def pairs(place, order, left, right, dots):
    n = left[0].shape[0]
    block = pltpu.VMEM((2, n, n), F32)
    outs = pl.pallas_call(
        functools.partial(pair_kernel, order),
        out_shape=(shaped(n // 2, n),) * (4 * len(order)),
        in_specs=[SMEM] + [HBM] * (len(left) + 1),
        out_specs=(VMEM,) * (4 * len(order)),
        scratch_shapes=[block, block, pltpu.SemaphoreType.DMA((2,)), pltpu.SemaphoreType.DMA],
        compiler_params=PARAMS,
        cost_estimate=cost(dots, n),
    )(place, *left, right)
    return groups(outs, 4)


def cross_kernel(place, mask, total, out, buffer, sem):
    here = Place(place)
    copy = pltpu.make_async_copy(total.at[here.zh], buffer, sem)
    copy.start()
    copy.wait()
    h = buffer.shape[0] // 2
    for i in range(2):
        for j in range(2):
            rows, cols = slice(i * h, (i + 1) * h), slice(j * h, (j + 1) * h)
            out[0, rows, cols] = -(buffer[rows, cols] * mask[0, i, j].astype(F32))


def cross_block(place, mask, total):
    n = total.shape[1]
    return pl.pallas_call(
        cross_kernel,
        out_shape=shaped(1, n, n),
        in_specs=[SMEM, SMEM, HBM],
        out_specs=VMEM,
        scratch_shapes=[pltpu.VMEM((n, n), F32), pltpu.SemaphoreType.DMA],
        compiler_params=SMALL,
        cost_estimate=light(n),
    )(place, mask, total)


def from_y(part, k):
    return lax.ppermute(part, "y", [(y, (y + k) % NY) for y in range(NY)])


def per_device(root_inverse, lower_panel, panel_mask, factor_inverse):
    place = jnp.stack([lax.axis_index(name) for name in AXES]).astype(jnp.int32)
    core, zh = lax.axis_index("core"), lax.axis_index("z_hi")
    away = swap(root_inverse, "z_hi")
    mine, turned = masked_block(panel_mask, lower_panel)

    good = core == zh
    kept, sent = jnp.where(good, root_inverse, away), jnp.where(good, away, root_inverse)
    piece = jnp.stack([kept, swap(sent, "core")])
    piece, mine, moved = lax.optimization_barrier((piece, mine, y_step(turned)))

    ring, rows_near, rows_far = [mine], [turned, moved], []
    had, totals = (0, 0), ()
    for r in range(NX):
        ends = [ring]
        ring.append(z_step(ring[-1]))
        if r == 0:
            back, ahead = from_y(piece, 1), from_y(piece, NY - 1)
            ring[1], back, ahead = lax.optimization_barrier((ring[1], back, ahead))
        if len(ring) < NZ:
            ring.append(z_step(ring[-1]))
        if r == 0:
            opposite = y_step(jnp.where(core == 0, back, ahead))
            groups_of = [[jnp.stack([piece, back])], [jnp.stack([opposite, ahead])]]
            groups_of[0].append(x_step(groups_of[0][0]))
        else:
            for group in groups_of:
                if len(group) < NX:
                    group.append(x_step(group[-1]))
            rows = rows_near if r == 1 else rows_far
            for _ in range(min(2, NY - len(rows))):
                rows.append(y_step(rows[-1]))
            ends.append(rows)
        ends += groups_of + ([rows_near] if r == 0 else [])
        values = [into[-1] for into in ends]
        if r == NX - 1:
            had = (NX - 1, NZ - 1)
            totals = accumulate(place, had, (0, 0), list(zip(*groups_of)), ring, totals)
            totals, values = lax.optimization_barrier((totals, values))
        else:
            values = lax.optimization_barrier(values)
        for into, value in zip(ends, values):
            into[-1] = value
        if r == 1:
            rows_far = [turned_block(ring[NL])]
    roots = list(zip(*groups_of))
    own, theirs = accumulate(place, (NX, NZ), had, roots, ring, totals)

    rows = rows_near + rows_far
    total, *outs = first_pairs(place, [NL - 1, NL - 2], rows, own, swap(theirs, "core"))
    cross = cross_block(place, panel_mask, total)
    out, *outs = groups(outs, 4)
    moving = [own + theirs for own, theirs in zip(out[2:], swap_both(out[:2]))]
    moving, total = lax.optimization_barrier((moving, total))
    moving = [z_step(half) for half in moving]
    outs += pairs(place, list(range(NL - 3, -1, -1)), rows, total, 0)
    for out in outs[:-1]:
        moving = [z_step(a + own + theirs) for a, own, theirs in zip(moving, out[2:], swap_both(out[:2]))]
    out = outs[-1]
    rest = [a + own + theirs for a, own, theirs in zip(moving, out[2:], swap_both(out[:2]))]
    return cross, factor_inverse + jnp.concatenate(rest, 0)[None]


def solution(mesh):
    split_mesh = Mesh(mesh.devices.reshape(NX, NL, 2, NH, NY), AXES)
    row = ("z_lo", "core")
    block = P("leaf", row, COL)
    return jax.shard_map(
        per_device,
        mesh=split_mesh,
        in_specs=(P(row, ("leaf",) + COL), block, block, block),
        out_specs=(block, block),
        check_vma=False,
    )
```

```python
import functools

import jax
import jax.numpy as jnp
from jax import lax
from jax.experimental import pallas as pl
from jax.experimental.pallas import tpu as pltpu
from jax.sharding import Mesh
from jax.sharding import PartitionSpec as P

AXES = ("leaf", "z_lo", "core", "z_hi", "y")
COL = ("z_hi", "y")
NX, NL, NH, NY = 4, 4, 2, 4
NZ = NL * NH
F32 = jnp.float32
HBM = pl.BlockSpec(memory_space=pltpu.HBM)
SMEM = pl.BlockSpec(memory_space=pltpu.SMEM)
VMEM = pl.BlockSpec(memory_space=pltpu.VMEM)
PARAMS = pltpu.CompilerParams(vmem_limit_bytes=56 << 20)
SMALL = pltpu.CompilerParams(vmem_limit_bytes=16 << 20)


def way(core):
    return 1 if core == 0 else -1


def z_step(block):
    def place(z, core):
        return ((z % NL) * 2 + core) * NH + z // NL

    pairs = [(place(z, core), place((z + way(core)) % NZ, core)) for z in range(NZ) for core in range(2)]
    return lax.ppermute(block, ("z_lo", "core", "z_hi"), pairs)


def y_step(block):
    pairs = [(core * NY + y, core * NY + (y + way(core)) % NY) for y in range(NY) for core in range(2)]
    return lax.ppermute(block, ("core", "y"), pairs)


def x_step(block):
    pairs = [(x * 2 + core, (x + way(core)) % NX * 2 + core) for x in range(NX) for core in range(2)]
    return lax.ppermute(block, ("leaf", "core"), pairs)


def swap(block, axis):
    return lax.ppermute(block, axis, [(0, 1), (1, 0)])


def swap_both(halves):
    return [swap(half, "core") for half in halves]


def split(value):
    high = value.astype(jnp.bfloat16)
    return high, (value - high.astype(F32)).astype(jnp.bfloat16)


def products(lefts, right):
    dot = functools.partial(jnp.dot, preferred_element_type=F32)
    right_high, right_low = split(right)
    outs = []
    for left in lefts:
        left_high, left_low = split(left)
        outs.append(dot(left_high, right_high) + (dot(left_high, right_low) + dot(left_low, right_high)))
    return outs


def cost(dots, n):
    return pl.CostEstimate(flops=6 * dots * n**3, bytes_accessed=12 * dots * n * n, transcendentals=0)


def light(n):
    return pl.CostEstimate(flops=n * n, bytes_accessed=12 * n * n, transcendentals=0)


def shaped(*shape):
    return jax.ShapeDtypeStruct(shape, F32)


class Place:
    def __init__(self, ref):
        self.x, self.zl, self.core, self.zh, self.y = (ref[i] for i in range(5))
        self.z = self.zh * NL + self.zl
        self.turn = 1 - 2 * self.core


def mask_kernel(mask, panel, out, turned):
    h = out.shape[0] // 2
    for i in range(2):
        for j in range(2):
            rows, cols = slice(i * h, (i + 1) * h), slice(j * h, (j + 1) * h)
            part = panel[0, rows, cols] * mask[0, i, j].astype(F32)
            out[rows, cols] = part
            turned[cols, rows] = part.T


def masked_block(mask, panel):
    n = panel.shape[1]
    return pl.pallas_call(
        mask_kernel,
        out_shape=(shaped(n, n), shaped(n, n)),
        in_specs=[SMEM, VMEM],
        out_specs=(VMEM, VMEM),
        compiler_params=SMALL,
        cost_estimate=light(n),
    )(mask, panel)


def turn_kernel(block, turned):
    turned[...] = block[...].T


def turned_block(block):
    n = block.shape[0]
    return pl.pallas_call(
        turn_kernel,
        out_shape=shaped(n, n),
        in_specs=[VMEM],
        out_specs=VMEM,
        compiler_params=SMALL,
        cost_estimate=light(n),
    )(block)


class Step:
    def __init__(self, here, have, had, c):
        self.arrival = have[0] - 1 - c // 2
        from_x = here.x - here.turn * self.arrival
        self.s = jnp.bitwise_and(here.turn * (here.z - from_x), NL - 1) + NL * lax.rem(c, 2)
        self.half = jnp.bitwise_and(here.z - here.turn * self.s, NZ - 1) // NL
        before = jnp.logical_and(self.arrival < had[0], self.s < had[1])
        self.ready = jnp.logical_and(self.s < have[1], jnp.logical_not(before))


class Gather:
    def __init__(self, here, have, had, roots, ring, buffers):
        self.here, self.have, self.had, self.roots, self.ring = here, have, had, roots, ring
        self.left_buffer, self.right_buffer, self.left_sems, self.right_sems = buffers

    def step(self, c):
        return Step(self.here, self.have, self.had, c)

    def start(self, c, slot):
        here, step = self.here, self.step(c)
        left, right = self.left_buffer, self.right_buffer

        @pl.when(step.ready)
        def _():
            for t, pieces in enumerate(self.roots):

                @pl.when(step.arrival == t)
                def _():
                    q = pieces[0].shape[3]
                    for p in range(NY):
                        at = pl.multiple_of(jnp.bitwise_and(here.y - p, NY - 1) * q, q)
                        source, to = pieces[p // 2].at[p % 2], left.at[slot, :, :, pl.ds(at, q)]
                        pltpu.make_async_copy(source, to, self.left_sems.at[slot]).start()

            for k, block in enumerate(self.ring):

                @pl.when(step.s == k)
                def _():
                    pltpu.make_async_copy(block, right.at[slot], self.right_sems.at[slot]).start()

    def run(self, totals):
        steps = 2 * self.have[0]

        @pl.loop(0, steps)
        def _(c):
            slot = lax.rem(c, 2)

            @pl.when(c + 1 < steps)
            def _():
                self.start(c + 1, 1 - slot)

            step = self.step(c)

            @pl.when(step.ready)
            def _():
                for buffer, sems in ((self.left_buffer, self.left_sems), (self.right_buffer, self.right_sems)):
                    pltpu.make_async_copy(buffer.at[slot], buffer.at[slot], sems.at[slot]).wait()
                left = self.left_buffer
                for total, out in zip(totals, products((left[slot, 0], left[slot, 1]), self.right_buffer[slot])):
                    total[step.half] = total[step.half] + out


class Pair:
    def __init__(self, here, left, buffer, sems):
        self.here, self.left, self.buffer, self.sems = here, left, buffer, sems

    def target(self, i):
        here = self.here
        own = lax.rem(i, 2)
        to_z = jnp.bitwise_and(here.z + here.turn * (2 * own - 1) * (i // 2), NZ - 1)
        return jnp.bitwise_and(to_z, NL - 1) * 2 + jnp.where(own == 1, here.core, 1 - here.core), to_z // NL

    def start(self, i):
        here = self.here
        block, _ = self.target(i)
        step = jnp.bitwise_and(here.turn * (here.y - jnp.bitwise_and(block, NY - 1)), NY - 1)
        index = jnp.where(block // NY == here.zh, step, step + NY)
        slot = lax.rem(i, 2)
        for k, ref in enumerate(self.left):

            @pl.when(index == k)
            def _():
                pltpu.make_async_copy(ref, self.buffer.at[slot], self.sems.at[slot]).start()

    def run(self, order, outs, total):
        first, last = 2 * order[0], 2 * order[-1]

        @pl.loop(0, 2 * len(order))
        def _(k):
            i = first - k // 2 * 2 + lax.rem(k, 2)
            slot = lax.rem(k, 2)
            pltpu.make_async_copy(self.buffer.at[slot], self.buffer.at[slot], self.sems.at[slot]).wait()
            (out,) = products((self.buffer[slot],), total[self.target(i)[1]])
            for j, (top, bottom) in enumerate(outs):
                h = top.shape[0]

                @pl.when(k == j)
                def _():
                    top[...] = out[:h]
                    bottom[...] = out[h:]

            @pl.when(i - 2 >= last)
            def _():
                self.start(i - 2)


def unpack(refs, sizes):
    parts = []
    for size in sizes:
        parts.append(refs[:size])
        refs = refs[size:]
    return parts + [refs]


def groups(refs, size):
    return [refs[i : i + size] for i in range(0, len(refs), size)]


def load(source, target, sem):
    copy = pltpu.make_async_copy(source, target, sem)
    copy.start()
    copy.wait()


def gather_kernel(have, had, place, *refs):
    roots, ring, before, afters, rest = unpack(refs, (2 * have[0], have[1], 2 if had[1] else 0, 2))
    left_buffer, right_buffer, own, theirs, left_sems, right_sems, sems = rest
    totals = (own, theirs)
    buffers = (left_buffer, right_buffer, left_sems, right_sems)
    gather = Gather(Place(place), have, had, groups(roots, 2), ring, buffers)
    gather.start(0, 0)
    loads = [pltpu.make_async_copy(ref, total, sems.at[k]) for k, (ref, total) in enumerate(zip(before, totals))]
    for copy in loads:
        copy.start()
    for copy in loads:
        copy.wait()
    if not loads:
        for total in totals:
            total[...] = jnp.zeros_like(total)
    gather.run(totals)
    stores = [pltpu.make_async_copy(total, ref, sems.at[k]) for k, (ref, total) in enumerate(zip(afters, totals))]
    for copy in stores:
        copy.start()
    for copy in stores:
        copy.wait()


def accumulate(place, have, had, roots, ring, totals):
    n = ring[0].shape[0]
    operands = [place] + [part for pieces in roots[: have[0]] for part in pieces]
    operands += ring[: have[1]]
    aliases = {}
    if had[1]:
        aliases = {len(operands): 0, len(operands) + 1: 1}
        operands += totals
    block = pltpu.VMEM((2, n, n), F32)
    pair = pltpu.SemaphoreType.DMA((2,))
    return pl.pallas_call(
        functools.partial(gather_kernel, have, had),
        out_shape=(shaped(2, n, n),) * 2,
        in_specs=[SMEM] + [HBM] * (len(operands) - 1),
        out_specs=(HBM,) * 2,
        scratch_shapes=[pltpu.VMEM((2, 2, n, n), F32), block, block, block, pair, pair, pair],
        input_output_aliases=aliases,
        compiler_params=PARAMS,
        cost_estimate=cost(6, n),
    )(*operands)


def first_kernel(order, place, *refs):
    left, (own, theirs, ancestor), outs, (buffer, total, extra, sems, total_sems) = unpack(refs, (2 * NY, 3, 4 * len(order)))
    pair = Pair(Place(place), left, buffer, sems)
    pair.start(2 * order[0])
    pair.start(2 * order[0] + 1)
    loads = [pltpu.make_async_copy(a, b, total_sems.at[k]) for k, (a, b) in enumerate(((own, total), (theirs, extra)))]
    for copy in loads:
        copy.start()
    for copy in loads:
        copy.wait()
    total[...] = total[...] + extra[...]
    store = pltpu.make_async_copy(total, ancestor, total_sems.at[0])
    store.start()
    pair.run(order, groups(outs, 2), total)
    store.wait()


def first_pairs(place, order, left, own, theirs):
    n = left[0].shape[0]
    block = pltpu.VMEM((2, n, n), F32)
    pair = pltpu.SemaphoreType.DMA((2,))

    def body(place, *refs):
        ins, outs = refs[: len(left) + 2], refs[len(left) + 2 :]
        first_kernel(order, place, *ins, *outs)

    return pl.pallas_call(
        body,
        out_shape=(shaped(2, n, n),) + (shaped(n // 2, n),) * (4 * len(order)),
        in_specs=[SMEM] + [HBM] * (len(left) + 2),
        out_specs=(HBM,) + (VMEM,) * (4 * len(order)),
        scratch_shapes=[block, block, block, pair, pair],
        compiler_params=PARAMS,
        cost_estimate=cost(2, n),
    )(place, *left, own, theirs)


def pair_kernel(order, place, *refs):
    left, (right,), outs, (buffer, total, sems, sem) = unpack(refs, (2 * NY, 1, 4 * len(order)))
    pair = Pair(Place(place), left, buffer, sems)
    pair.start(2 * order[0])
    pair.start(2 * order[0] + 1)
    load(right, total, sem)
    pair.run(order, groups(outs, 2), total)


def pairs(place, order, left, right, dots):
    n = left[0].shape[0]
    block = pltpu.VMEM((2, n, n), F32)
    outs = pl.pallas_call(
        functools.partial(pair_kernel, order),
        out_shape=(shaped(n // 2, n),) * (4 * len(order)),
        in_specs=[SMEM] + [HBM] * (len(left) + 1),
        out_specs=(VMEM,) * (4 * len(order)),
        scratch_shapes=[block, block, pltpu.SemaphoreType.DMA((2,)), pltpu.SemaphoreType.DMA],
        compiler_params=PARAMS,
        cost_estimate=cost(dots, n),
    )(place, *left, right)
    return groups(outs, 4)


def cross_kernel(place, mask, total, out, buffer, sem):
    here = Place(place)
    copy = pltpu.make_async_copy(total.at[here.zh], buffer, sem)
    copy.start()
    copy.wait()
    h = buffer.shape[0] // 2
    for i in range(2):
        for j in range(2):
            rows, cols = slice(i * h, (i + 1) * h), slice(j * h, (j + 1) * h)
            out[0, rows, cols] = -(buffer[rows, cols] * mask[0, i, j].astype(F32))


def cross_block(place, mask, total):
    n = total.shape[1]
    return pl.pallas_call(
        cross_kernel,
        out_shape=shaped(1, n, n),
        in_specs=[SMEM, SMEM, HBM],
        out_specs=VMEM,
        scratch_shapes=[pltpu.VMEM((n, n), F32), pltpu.SemaphoreType.DMA],
        compiler_params=SMALL,
        cost_estimate=light(n),
    )(place, mask, total)


def from_y(part, k):
    return lax.ppermute(part, "y", [(y, (y + k) % NY) for y in range(NY)])


def per_device(root_inverse, lower_panel, panel_mask, factor_inverse):
    place = jnp.stack([lax.axis_index(name) for name in AXES]).astype(jnp.int32)
    core, zh = lax.axis_index("core"), lax.axis_index("z_hi")
    away = swap(root_inverse, "z_hi")
    mine, turned = masked_block(panel_mask, lower_panel)

    good = core == zh
    kept, sent = jnp.where(good, root_inverse, away), jnp.where(good, away, root_inverse)
    piece = jnp.stack([kept, swap(sent, "core")])
    piece, mine, moved = lax.optimization_barrier((piece, mine, y_step(turned)))

    ring, rows_near, rows_far = [mine], [turned, moved], []
    had, totals = (0, 0), ()
    for r in range(NX):
        ends = [ring]
        ring.append(z_step(ring[-1]))
        if r == 0:
            back, ahead = from_y(piece, 1), from_y(piece, NY - 1)
            ring[1], back, ahead = lax.optimization_barrier((ring[1], back, ahead))
        if len(ring) < NZ:
            ring.append(z_step(ring[-1]))
        if r == 0:
            opposite = y_step(jnp.where(core == 0, back, ahead))
            groups_of = [[jnp.stack([piece, back])], [jnp.stack([opposite, ahead])]]
            groups_of[0].append(x_step(groups_of[0][0]))
        else:
            for group in groups_of:
                if len(group) < NX:
                    group.append(x_step(group[-1]))
            rows = rows_near if r == 1 else rows_far
            for _ in range(min(2, NY - len(rows))):
                rows.append(y_step(rows[-1]))
            ends.append(rows)
        ends += groups_of + ([rows_near] if r == 0 else [])
        values = [into[-1] for into in ends]
        if r >= 2:
            have = (r, 2 * r + 1)
            totals = accumulate(place, have, had, list(zip(*groups_of)), ring, totals)
            had = have
            totals, values = lax.optimization_barrier((totals, values))
        else:
            values = lax.optimization_barrier(values)
        for into, value in zip(ends, values):
            into[-1] = value
        if r == 1:
            rows_far = [turned_block(ring[NL])]
    roots = list(zip(*groups_of))
    own, theirs = accumulate(place, (NX, NZ), had, roots, ring, totals)

    rows = rows_near + rows_far
    total, *outs = first_pairs(place, [NL - 1, NL - 2], rows, own, swap(theirs, "core"))
    cross = cross_block(place, panel_mask, total)
    out, *outs = groups(outs, 4)
    moving = [own + theirs for own, theirs in zip(out[2:], swap_both(out[:2]))]
    moving, total = lax.optimization_barrier((moving, total))
    moving = [z_step(half) for half in moving]
    outs += pairs(place, list(range(NL - 3, -1, -1)), rows, total, 0)
    for out in outs[:-1]:
        moving = [z_step(a + own + theirs) for a, own, theirs in zip(moving, out[2:], swap_both(out[:2]))]
    out = outs[-1]
    rest = [a + own + theirs for a, own, theirs in zip(moving, out[2:], swap_both(out[:2]))]
    return cross, factor_inverse + jnp.concatenate(rest, 0)[None]


def solution(mesh):
    split_mesh = Mesh(mesh.devices.reshape(NX, NL, 2, NH, NY), AXES)
    row = ("z_lo", "core")
    block = P("leaf", row, COL)
    return jax.shard_map(
        per_device,
        mesh=split_mesh,
        in_specs=(P(row, ("leaf",) + COL), block, block, block),
        out_specs=(block, block),
        check_vma=False,
    )
```

```python
import functools

import jax
import jax.numpy as jnp
from jax import lax
from jax.experimental import pallas as pl
from jax.experimental.pallas import tpu as pltpu
from jax.sharding import Mesh
from jax.sharding import PartitionSpec as P

AXES = ("leaf", "z_lo", "core", "z_hi", "y")
COL = ("z_hi", "y")
NX, NL, NH, NY = 4, 4, 2, 4
NZ = NL * NH
F32 = jnp.float32
HBM = pl.BlockSpec(memory_space=pltpu.HBM)
SMEM = pl.BlockSpec(memory_space=pltpu.SMEM)
VMEM = pl.BlockSpec(memory_space=pltpu.VMEM)
PARAMS = pltpu.CompilerParams(vmem_limit_bytes=56 << 20)
MIDDLE = pltpu.CompilerParams(vmem_limit_bytes=40 << 20)
SMALL = pltpu.CompilerParams(vmem_limit_bytes=16 << 20)


def way(core):
    return 1 if core == 0 else -1


def z_step(block):
    def place(z, core):
        return ((z % NL) * 2 + core) * NH + z // NL

    pairs = [(place(z, core), place((z + way(core)) % NZ, core)) for z in range(NZ) for core in range(2)]
    return lax.ppermute(block, ("z_lo", "core", "z_hi"), pairs)


def y_step(block):
    pairs = [(core * NY + y, core * NY + (y + way(core)) % NY) for y in range(NY) for core in range(2)]
    return lax.ppermute(block, ("core", "y"), pairs)


def x_step(block):
    pairs = [(x * 2 + core, (x + way(core)) % NX * 2 + core) for x in range(NX) for core in range(2)]
    return lax.ppermute(block, ("leaf", "core"), pairs)


def swap(block, axis):
    return lax.ppermute(block, axis, [(0, 1), (1, 0)])


def swap_both(halves):
    return [swap(half, "core") for half in halves]


def split(value):
    high = value.astype(jnp.bfloat16)
    return high, (value - high.astype(F32)).astype(jnp.bfloat16)


def products(lefts, right):
    dot = functools.partial(jnp.dot, preferred_element_type=F32)
    right_high, right_low = split(right)
    outs = []
    for left in lefts:
        left_high, left_low = split(left)
        outs.append(dot(left_high, right_high) + (dot(left_high, right_low) + dot(left_low, right_high)))
    return outs


def cost(dots, n):
    return pl.CostEstimate(flops=6 * dots * n**3, bytes_accessed=12 * dots * n * n, transcendentals=0)


def light(n):
    return pl.CostEstimate(flops=n * n, bytes_accessed=12 * n * n, transcendentals=0)


def shaped(*shape):
    return jax.ShapeDtypeStruct(shape, F32)


class Place:
    def __init__(self, ref):
        self.x, self.zl, self.core, self.zh, self.y = (ref[i] for i in range(5))
        self.z = self.zh * NL + self.zl
        self.turn = 1 - 2 * self.core


def mask_kernel(mask, panel, out, turned):
    h = out.shape[0] // 2
    for i in range(2):
        for j in range(2):
            rows, cols = slice(i * h, (i + 1) * h), slice(j * h, (j + 1) * h)
            part = panel[0, rows, cols] * mask[0, i, j].astype(F32)
            out[rows, cols] = part
            turned[cols, rows] = part.T


def masked_block(mask, panel):
    n = panel.shape[1]
    return pl.pallas_call(
        mask_kernel,
        out_shape=(shaped(n, n), shaped(n, n)),
        in_specs=[SMEM, VMEM],
        out_specs=(VMEM, VMEM),
        compiler_params=SMALL,
        cost_estimate=light(n),
    )(mask, panel)


def turn_kernel(block, turned):
    turned[...] = block[...].T


def turned_block(block):
    n = block.shape[0]
    return pl.pallas_call(
        turn_kernel,
        out_shape=shaped(n, n),
        in_specs=[VMEM],
        out_specs=VMEM,
        compiler_params=SMALL,
        cost_estimate=light(n),
    )(block)


class Step:
    def __init__(self, here, have, had, c):
        self.arrival = have[0] - 1 - c // 2
        from_x = here.x - here.turn * self.arrival
        self.s = jnp.bitwise_and(here.turn * (here.z - from_x), NL - 1) + NL * lax.rem(c, 2)
        self.half = jnp.bitwise_and(here.z - here.turn * self.s, NZ - 1) // NL
        before = jnp.logical_and(self.arrival < had[0], self.s < had[1])
        self.ready = jnp.logical_and(self.s < have[1], jnp.logical_not(before))


class Gather:
    def __init__(self, here, have, had, roots, ring, buffers):
        self.here, self.have, self.had, self.roots, self.ring = here, have, had, roots, ring
        self.left_buffer, self.right_buffer, self.left_sems, self.right_sems = buffers

    def step(self, c):
        return Step(self.here, self.have, self.had, c)

    def start(self, c, slot):
        here, step = self.here, self.step(c)
        left, right = self.left_buffer, self.right_buffer

        @pl.when(step.ready)
        def _():
            for t, pieces in enumerate(self.roots):

                @pl.when(step.arrival == t)
                def _():
                    q = pieces[0].shape[3]
                    for p in range(NY):
                        at = pl.multiple_of(jnp.bitwise_and(here.y - p, NY - 1) * q, q)
                        source, to = pieces[p // 2].at[p % 2], left.at[slot, :, :, pl.ds(at, q)]
                        pltpu.make_async_copy(source, to, self.left_sems.at[slot]).start()

            for k, block in enumerate(self.ring):

                @pl.when(step.s == k)
                def _():
                    pltpu.make_async_copy(block, right.at[slot], self.right_sems.at[slot]).start()

    def run(self, totals):
        steps = 2 * self.have[0]

        @pl.loop(0, steps)
        def _(c):
            slot = lax.rem(c, 2)

            @pl.when(c + 1 < steps)
            def _():
                self.start(c + 1, 1 - slot)

            step = self.step(c)

            @pl.when(step.ready)
            def _():
                for buffer, sems in ((self.left_buffer, self.left_sems), (self.right_buffer, self.right_sems)):
                    pltpu.make_async_copy(buffer.at[slot], buffer.at[slot], sems.at[slot]).wait()
                left = self.left_buffer
                for total, out in zip(totals, products((left[slot, 0], left[slot, 1]), self.right_buffer[slot])):
                    total[step.half] = total[step.half] + out


class Pair:
    def __init__(self, here, left, buffer, sems):
        self.here, self.left, self.buffer, self.sems = here, left, buffer, sems

    def target(self, i):
        here = self.here
        own = lax.rem(i, 2)
        to_z = jnp.bitwise_and(here.z + here.turn * (2 * own - 1) * (i // 2), NZ - 1)
        return jnp.bitwise_and(to_z, NL - 1) * 2 + jnp.where(own == 1, here.core, 1 - here.core), to_z // NL

    def start(self, i):
        here = self.here
        block, _ = self.target(i)
        step = jnp.bitwise_and(here.turn * (here.y - jnp.bitwise_and(block, NY - 1)), NY - 1)
        index = jnp.where(block // NY == here.zh, step, step + NY)
        slot = lax.rem(i, 2)
        for k, ref in enumerate(self.left):

            @pl.when(index == k)
            def _():
                pltpu.make_async_copy(ref, self.buffer.at[slot], self.sems.at[slot]).start()

    def run(self, order, outs, total):
        first, last = 2 * order[0], 2 * order[-1]

        @pl.loop(0, 2 * len(order))
        def _(k):
            i = first - k // 2 * 2 + lax.rem(k, 2)
            slot = lax.rem(k, 2)
            pltpu.make_async_copy(self.buffer.at[slot], self.buffer.at[slot], self.sems.at[slot]).wait()
            (out,) = products((self.buffer[slot],), total[self.target(i)[1]])
            for j, (top, bottom) in enumerate(outs):
                h = top.shape[0]

                @pl.when(k == j)
                def _():
                    top[...] = out[:h]
                    bottom[...] = out[h:]

            @pl.when(i - 2 >= last)
            def _():
                self.start(i - 2)


def unpack(refs, sizes):
    parts = []
    for size in sizes:
        parts.append(refs[:size])
        refs = refs[size:]
    return parts + [refs]


def groups(refs, size):
    return [refs[i : i + size] for i in range(0, len(refs), size)]


def load(source, target, sem):
    copy = pltpu.make_async_copy(source, target, sem)
    copy.start()
    copy.wait()


def gather_kernel(have, had, place, *refs):
    roots, ring, before, afters, rest = unpack(refs, (2 * have[0], have[1], 2 if had[1] else 0, 2))
    left_buffer, right_buffer, own, theirs, left_sems, right_sems, sems = rest
    totals = (own, theirs)
    buffers = (left_buffer, right_buffer, left_sems, right_sems)
    gather = Gather(Place(place), have, had, groups(roots, 2), ring, buffers)
    gather.start(0, 0)
    loads = [pltpu.make_async_copy(ref, total, sems.at[k]) for k, (ref, total) in enumerate(zip(before, totals))]
    for copy in loads:
        copy.start()
    for copy in loads:
        copy.wait()
    if not loads:
        for total in totals:
            total[...] = jnp.zeros_like(total)
    gather.run(totals)
    stores = [pltpu.make_async_copy(total, ref, sems.at[k]) for k, (ref, total) in enumerate(zip(afters, totals))]
    for copy in stores:
        copy.start()
    for copy in stores:
        copy.wait()


def accumulate(place, have, had, roots, ring, totals):
    n = ring[0].shape[0]
    operands = [place] + [part for pieces in roots[: have[0]] for part in pieces]
    operands += ring[: have[1]]
    aliases = {}
    if had[1]:
        aliases = {len(operands): 0, len(operands) + 1: 1}
        operands += totals
    block = pltpu.VMEM((2, n, n), F32)
    pair = pltpu.SemaphoreType.DMA((2,))
    return pl.pallas_call(
        functools.partial(gather_kernel, have, had),
        out_shape=(shaped(2, n, n),) * 2,
        in_specs=[SMEM] + [HBM] * (len(operands) - 1),
        out_specs=(HBM,) * 2,
        scratch_shapes=[pltpu.VMEM((2, 2, n, n), F32), block, block, block, pair, pair, pair],
        input_output_aliases=aliases,
        compiler_params=PARAMS,
        cost_estimate=cost(6, n),
    )(*operands)


def first_kernel(order, place, *refs):
    left, (own, theirs, ancestor), outs, (buffer, total, extra, sems, total_sems) = unpack(refs, (2 * NY, 3, 4 * len(order)))
    pair = Pair(Place(place), left, buffer, sems)
    pair.start(2 * order[0])
    pair.start(2 * order[0] + 1)
    loads = [pltpu.make_async_copy(a, b, total_sems.at[k]) for k, (a, b) in enumerate(((own, total), (theirs, extra)))]
    for copy in loads:
        copy.start()
    for copy in loads:
        copy.wait()
    total[...] = total[...] + extra[...]
    store = pltpu.make_async_copy(total, ancestor, total_sems.at[0])
    store.start()
    pair.run(order, groups(outs, 2), total)
    store.wait()


def first_pairs(place, order, left, own, theirs):
    n = left[0].shape[0]
    block = pltpu.VMEM((2, n, n), F32)
    pair = pltpu.SemaphoreType.DMA((2,))

    def body(place, *refs):
        ins, outs = refs[: len(left) + 2], refs[len(left) + 2 :]
        first_kernel(order, place, *ins, *outs)

    return pl.pallas_call(
        body,
        out_shape=(shaped(2, n, n),) + (shaped(n // 2, n),) * (4 * len(order)),
        in_specs=[SMEM] + [HBM] * (len(left) + 2),
        out_specs=(HBM,) + (VMEM,) * (4 * len(order)),
        scratch_shapes=[block, block, block, pair, pair],
        compiler_params=MIDDLE,
        cost_estimate=cost(2, n),
    )(place, *left, own, theirs)


def pair_kernel(order, place, *refs):
    left, (right,), outs, (buffer, total, sems, sem) = unpack(refs, (2 * NY, 1, 4 * len(order)))
    pair = Pair(Place(place), left, buffer, sems)
    pair.start(2 * order[0])
    pair.start(2 * order[0] + 1)
    load(right, total, sem)
    pair.run(order, groups(outs, 2), total)


def pairs(place, order, left, right, dots):
    n = left[0].shape[0]
    block = pltpu.VMEM((2, n, n), F32)
    outs = pl.pallas_call(
        functools.partial(pair_kernel, order),
        out_shape=(shaped(n // 2, n),) * (4 * len(order)),
        in_specs=[SMEM] + [HBM] * (len(left) + 1),
        out_specs=(VMEM,) * (4 * len(order)),
        scratch_shapes=[block, block, pltpu.SemaphoreType.DMA((2,)), pltpu.SemaphoreType.DMA],
        compiler_params=MIDDLE,
        cost_estimate=cost(dots, n),
    )(place, *left, right)
    return groups(outs, 4)


def cross_kernel(place, mask, total, out, buffer, sem):
    here = Place(place)
    copy = pltpu.make_async_copy(total.at[here.zh], buffer, sem)
    copy.start()
    copy.wait()
    h = buffer.shape[0] // 2
    for i in range(2):
        for j in range(2):
            rows, cols = slice(i * h, (i + 1) * h), slice(j * h, (j + 1) * h)
            out[0, rows, cols] = -(buffer[rows, cols] * mask[0, i, j].astype(F32))


def cross_block(place, mask, total):
    n = total.shape[1]
    return pl.pallas_call(
        cross_kernel,
        out_shape=shaped(1, n, n),
        in_specs=[SMEM, SMEM, HBM],
        out_specs=VMEM,
        scratch_shapes=[pltpu.VMEM((n, n), F32), pltpu.SemaphoreType.DMA],
        compiler_params=SMALL,
        cost_estimate=light(n),
    )(place, mask, total)


def from_y(part, k):
    return lax.ppermute(part, "y", [(y, (y + k) % NY) for y in range(NY)])


def per_device(root_inverse, lower_panel, panel_mask, factor_inverse):
    place = jnp.stack([lax.axis_index(name) for name in AXES]).astype(jnp.int32)
    core, zh = lax.axis_index("core"), lax.axis_index("z_hi")
    away = swap(root_inverse, "z_hi")
    mine, turned = masked_block(panel_mask, lower_panel)

    good = core == zh
    kept, sent = jnp.where(good, root_inverse, away), jnp.where(good, away, root_inverse)
    piece = jnp.stack([kept, swap(sent, "core")])
    piece, mine, moved = lax.optimization_barrier((piece, mine, y_step(turned)))

    ring, rows_near, rows_far = [mine], [turned, moved], []
    had, totals = (0, 0), ()
    for r in range(NX):
        ends = [ring]
        ring.append(z_step(ring[-1]))
        if r == 0:
            back, ahead = from_y(piece, 1), from_y(piece, NY - 1)
            ring[1], back, ahead = lax.optimization_barrier((ring[1], back, ahead))
        if len(ring) < NZ:
            ring.append(z_step(ring[-1]))
        if r == 0:
            opposite = y_step(jnp.where(core == 0, back, ahead))
            groups_of = [[jnp.stack([piece, back])], [jnp.stack([opposite, ahead])]]
            groups_of[0].append(x_step(groups_of[0][0]))
        else:
            for group in groups_of:
                if len(group) < NX:
                    group.append(x_step(group[-1]))
            rows = rows_near if r == 1 else rows_far
            for _ in range(min(2, NY - len(rows))):
                rows.append(y_step(rows[-1]))
            ends.append(rows)
        ends += groups_of + ([rows_near] if r == 0 else [])
        values = [into[-1] for into in ends]
        if r == NX - 1:
            had = (NX - 1, NZ - 1)
            totals = accumulate(place, had, (0, 0), list(zip(*groups_of)), ring, totals)
            totals, values = lax.optimization_barrier((totals, values))
        else:
            values = lax.optimization_barrier(values)
        for into, value in zip(ends, values):
            into[-1] = value
        if r == 1:
            rows_far = [turned_block(ring[NL])]
    roots = list(zip(*groups_of))
    own, theirs = accumulate(place, (NX, NZ), had, roots, ring, totals)

    rows = rows_near + rows_far
    total, *outs = first_pairs(place, [NL - 1, NL - 2], rows, own, swap(theirs, "core"))
    cross = cross_block(place, panel_mask, total)
    out, *outs = groups(outs, 4)
    moving = [own + theirs for own, theirs in zip(out[2:], swap_both(out[:2]))]
    moving, total = lax.optimization_barrier((moving, total))
    moving = [z_step(half) for half in moving]
    outs += pairs(place, list(range(NL - 3, -1, -1)), rows, total, 0)
    for out in outs[:-1]:
        moving = [z_step(a + own + theirs) for a, own, theirs in zip(moving, out[2:], swap_both(out[:2]))]
    out = outs[-1]
    rest = [a + own + theirs for a, own, theirs in zip(moving, out[2:], swap_both(out[:2]))]
    return cross, factor_inverse + jnp.concatenate(rest, 0)[None]


def solution(mesh):
    split_mesh = Mesh(mesh.devices.reshape(NX, NL, 2, NH, NY), AXES)
    row = ("z_lo", "core")
    block = P("leaf", row, COL)
    return jax.shard_map(
        per_device,
        mesh=split_mesh,
        in_specs=(P(row, ("leaf",) + COL), block, block, block),
        out_specs=(block, block),
        check_vma=False,
    )
```
